32 devices in a mesh: fsdp: 8 (over z, x), side: 4 (over y, core).
Axes of the slice: x: 2, y: 2, z: 4, core: 2. Of those that a mesh axis runs over, the one named last changes fastest.
Arguments:
- attn_inputs: bfloat16 [4096, 5120], P(('side', 'fsdp')), may hold values from -6 to 6
- queries: bfloat16 [4096, 2560], P(('side', 'fsdp')), may hold values from -310 to 310
- key_vectors: bfloat16 [4096, 512], P(('side', 'fsdp')), may hold values from -12 to 12
- logp_grad: bfloat16 [4096, 2560], P(('side', 'fsdp')), may hold values from -24 to 24
- new_logp: float32 [4096], P(('side', 'fsdp')), may hold values from -6.5 to -0.01
- old_logp: float32 [4096], P(('side', 'fsdp')), may hold values from -4 to -0.05
- rewards: float32 [8], replicated, may hold values from -8 to 8
- group_ids: int32 [8], replicated, may hold values from 0 to 1
- lengths: int32 [8], replicated, may hold values from 256 to 512
- value_proj: bfloat16 [5120, 512], P('fsdp'), may hold values from -0.078125 to 0.078125
- first_moment: bfloat16 [5120, 512], P(('fsdp', 'side')), may hold values from -120 to 120
- second_moment: bfloat16 [5120, 512], P(('fsdp', 'side')), may hold values from 100 to 9984
Outputs:
- input_grad: bfloat16 [4096, 5120], P(('side', 'fsdp'))
- new_proj: bfloat16 [5120, 512], P('fsdp')
- new_first: bfloat16 [5120, 512], P(('fsdp', 'side'))
- new_second: bfloat16 [5120, 512], P(('fsdp', 'side'))
The draws below stay inside these ranges and needn't reach their ends.
All inputs are finite; a program needn't handle non-finite values.
Results may differ from the reference program's by a relative error of at most 0.03.
Values may be sent and summed in bfloat16 or wider, within the bound.
No kernel may reach another device: no remote copies, remote signals or barrier semaphores. Data moves between devices by JAX's collectives and lax.ppermute only.
A program may use at most 64 MiB of HBM per device.

```python
import math
import jax
import jax.numpy as jnp
from jax import lax

D = 5120
QH = 20
KVH = 4
HEAD = 128
ROLLS = 2
TOK_DEV = 128
LENGTH = 512
TOKENS = 1024
ALLROLL = 8
ALLTOK = 4096
GROUPS = 2
N_FSDP = 8
N_SIDE = 4


def attention_pair(key):
    base = jax.random.fold_in(key, 11)
    key_one, key_two = jax.random.split(base, 2)
    keys_drawn = jnp.clip(jax.random.normal(key_one, (ALLTOK, KVH * HEAD), jnp.float32), -6.0, 6.0)
    query_drawn = jnp.clip(jax.random.normal(key_two, (ALLTOK, QH * HEAD), jnp.float32), -6.0, 6.0)
    return (query_drawn, keys_drawn)


def log_probs(key):
    base = jax.random.fold_in(key, 23)
    key_one, key_two = jax.random.split(base, 2)
    old_value = jax.random.uniform(key_one, (ALLTOK,), jnp.float32, -4.0, -0.05)
    noise = jnp.clip(jax.random.normal(key_two, (ALLTOK,), jnp.float32), -4.0, 4.0)
    new_value = jnp.minimum(old_value + 0.3 * noise, -0.01)
    return (new_value, old_value)


def draw_queries(key, part):
    return attention_pair(key)[0].astype(jnp.bfloat16)


def draw_key_vectors(key, part):
    return attention_pair(key)[1].astype(jnp.bfloat16)


def draw_new_logp(key, part):
    return log_probs(key)[0]


def draw_old_logp(key, part):
    return log_probs(key)[1]


def with_ends(values, rng, low, largest):
    longest = values.shape.index(max(values.shape))
    spots = []
    for shift in (0, 1):
        where = [jax.random.randint(jax.random.fold_in(rng, axis), (), 0, length) for axis, length in enumerate(values.shape)]
        where[longest] = (where[longest] + shift) % values.shape[longest]
        spots.append(tuple(where))
    return values.at[spots[0]].set(low).at[spots[1]].set(largest)


def strengthened(entries, stream_key, source, target, blocks, factor):
    def block_of(dim):
        return (jnp.arange(entries.shape[dim]) // (entries.shape[dim] // blocks)).reshape((-1,) + (1,) * (entries.ndim - 1 - dim))

    one_side = jax.random.permutation(stream_key, blocks)[block_of(target)]
    far = (block_of(target) + blocks // 2) % blocks
    return jnp.where((block_of(source) == one_side) | (block_of(source) == far), factor * entries, entries)


def block_scale(own_key, shape, shards, low, high):
    gain, own = 1.0, jax.random.fold_in(own_key, 6)
    for dim, shards_of in shards:
        steps = jnp.exp(jax.random.uniform(jax.random.fold_in(own, dim), (shards_of,), jnp.float32, low / len(shards), high / len(shards)))
        gain = gain * jnp.repeat(steps, shape[dim] // shards_of).reshape([-1 if axis == dim else 1 for axis in range(len(shape))])
    return gain


def bell_draw(own_key, extent, deviation, bound, cuts=(), kind=jnp.bfloat16):
    values = deviation * jax.random.normal(own_key, extent, jnp.float32)
    if cuts:
        values = values * block_scale(own_key, extent, cuts, -0.22, 0.18)
    return jnp.clip(values, -bound, bound).astype(kind)


def noise_with(rng, dims, scale, bound, cuts, heavy, kind=jnp.bfloat16):
    entries = scale * jax.random.normal(rng, dims, jnp.float32)
    if cuts:
        entries = entries * block_scale(rng, dims, cuts, -0.22, 0.18)
    return jnp.clip(strengthened(entries, jax.random.fold_in(rng, 3), *heavy), -bound, bound).astype(kind)


def setup_inputs(seed: int = 0) -> dict:
    seeds = jax.random.split(jax.random.key(seed), 13)
    attn_inputs = noise_with(seeds[0], (ALLTOK, D), 1.0, 6.0, ((0, 32),), (0, 1, 32, 2.75))
    queries = draw_queries(jax.random.fold_in(seeds[12], 71), 0)
    key_vectors = draw_key_vectors(jax.random.fold_in(seeds[12], 71), 0)
    logp_grad = bell_draw(seeds[3], (ALLTOK, QH * HEAD), 4.0, 24.0, ((0, 32),))
    new_logp = draw_new_logp(jax.random.fold_in(seeds[12], 71), 0)
    old_logp = draw_old_logp(jax.random.fold_in(seeds[12], 71), 0)
    rewards = bell_draw(seeds[6], (ALLROLL,), 2.0, 8.0, (), jnp.float32)
    group_ids = with_ends(jax.random.randint(seeds[7], (ALLROLL,), 0, GROUPS), jax.random.fold_in(seeds[7], 1), 0, GROUPS - 1).astype(jnp.int32)
    lengths = with_ends(jax.random.randint(seeds[8], (ALLROLL,), LENGTH // 2, LENGTH + 1), jax.random.fold_in(seeds[8], 1), LENGTH // 2, LENGTH).astype(jnp.int32)
    value_proj = bell_draw(seeds[9], (D, KVH * HEAD), D ** -0.5, 0.078125, ((0, 8),))
    first_moment = bell_draw(seeds[10], (D, KVH * HEAD), 20.0, 120.0, ((0, 32),))
    second_moment = jnp.clip(jnp.exp(math.log(9984.0) - 4.603569 * jax.random.uniform(seeds[11], (D, KVH * HEAD), jnp.float32) ** block_scale(seeds[11], (D, KVH * HEAD), ((0, 32),), -0.2, 0.2)), 100.0, 9984.0).astype(jnp.bfloat16)
    return {"attn_inputs": attn_inputs, "queries": queries, "key_vectors": key_vectors, "logp_grad": logp_grad, "new_logp": new_logp, "old_logp": old_logp, "rewards": rewards, "group_ids": group_ids, "lengths": lengths, "value_proj": value_proj, "first_moment": first_moment, "second_moment": second_moment}


clip_low = 0.8
clip_high = 1.2
decay_first = 0.9
decay_second = 0.95
step_rate = 0.001
weight_decay = 0.1
adam_eps = 1e-08
bias_first = 1.0 - 0.9 ** 10
bias_second = 1.0 - 0.95 ** 10

def advantages(rewards, group_ids):
    group_count = rewards.shape[0] // 4
    member = (group_ids[:, None] == jnp.arange(group_count, dtype=jnp.int32)[None, :]).astype(jnp.float32)
    counts = jnp.maximum(lax.optimization_barrier(jnp.sum(member, axis=0)), 1.0)
    group_mean = lax.optimization_barrier(jnp.sum(member * rewards[:, None], axis=0)) / counts
    own_mean = lax.optimization_barrier(jnp.sum(member * group_mean[None, :], axis=1))
    spread = rewards - own_mean
    variance = lax.optimization_barrier(jnp.sum(member * (spread * spread)[:, None], axis=0)) / counts
    own_std = jnp.sqrt(lax.optimization_barrier(jnp.sum(member * variance[None, :], axis=1)))
    return spread / jnp.maximum(own_std, 1.0)

def coefficient(new_lp, old_lp, adv_tok, len_tok, pos_tok, full_len):
    ratio_now = jnp.exp(new_lp - old_lp)
    clipped = jnp.clip(ratio_now, clip_low, clip_high)
    active = (ratio_now * adv_tok <= clipped * adv_tok) & (pos_tok < len_tok)
    len_weight = full_len / len_tok.astype(jnp.float32)
    return jnp.where(active, -adv_tok * ratio_now * len_weight, 0.0)

def block_values(query_blk, grad_blk, roll_keys, first_pos):
    tok_rows = query_blk.shape[0]
    key_count = roll_keys.shape[0]
    per_group = QH // KVH
    score_scale = 1.0 / math.sqrt(HEAD)
    query_pos = first_pos + jnp.arange(tok_rows, dtype=jnp.int32)
    key_pos = jnp.arange(key_count, dtype=jnp.int32)
    allowed = jnp.tile(key_pos[None, :] <= query_pos[:, None], (per_group, 1))
    pieces = []
    for kv_head in range(KVH):
        col_low = kv_head * per_group * HEAD
        col_high = col_low + per_group * HEAD
        q_part = query_blk[:, col_low:col_high].reshape(tok_rows, per_group, HEAD).transpose(1, 0, 2).reshape(per_group * tok_rows, HEAD)
        g_part = grad_blk[:, col_low:col_high].reshape(tok_rows, per_group, HEAD).transpose(1, 0, 2).reshape(per_group * tok_rows, HEAD)
        k_part = roll_keys[:, kv_head * HEAD:(kv_head + 1) * HEAD]
        scores = jnp.dot(q_part, k_part.T, preferred_element_type=jnp.float32) * score_scale
        scores = jnp.where(allowed, scores, -1e+30)
        top_val = lax.optimization_barrier(jnp.max(scores, axis=1, keepdims=True))
        expo = jnp.exp(scores - top_val)
        attention = (expo / lax.optimization_barrier(jnp.sum(expo, axis=1, keepdims=True))).astype(jnp.bfloat16)
        pieces.append(jnp.dot(attention.T, g_part, preferred_element_type=jnp.float32))
    return jnp.concatenate(pieces, axis=1)

def adam_rows(old_rows, grad_rows, first_moment, second_moment):
    first = decay_first * first_moment.astype(jnp.float32) + (1.0 - decay_first) * grad_rows
    second = decay_second * second_moment.astype(jnp.float32) + (1.0 - decay_second) * grad_rows * grad_rows
    weight_now = old_rows.astype(jnp.float32)
    update = first / bias_first / (jnp.sqrt(second / bias_second) + adam_eps) + weight_decay * weight_now
    return ((weight_now - step_rate * update).astype(jnp.bfloat16), first.astype(jnp.bfloat16), second.astype(jnp.bfloat16))

def to_rollouts(array):
    half = TOK_DEV // ROLLS
    width = array.shape[1]
    shaped = array.reshape(N_SIDE, N_FSDP, ROLLS, half, width).transpose(0, 2, 1, 3, 4)
    return shaped.reshape(ALLROLL, N_FSDP, half, width)

def reference(attn_inputs, queries, key_vectors, logp_grad, new_logp, old_logp, rewards, group_ids, lengths, value_proj, first_moment, second_moment):
    half = TOK_DEV // ROLLS
    advantage = advantages(rewards, group_ids)
    token_ids = jnp.arange(ALLTOK, dtype=jnp.int32)
    copy_index = token_ids // TOKENS
    block_index = token_ids // TOK_DEV % N_FSDP
    slot = token_ids % TOK_DEV
    roll_index = copy_index * ROLLS + slot // half
    position = block_index * half + slot % half
    coeff = coefficient(new_logp, old_logp, advantage[roll_index], lengths[roll_index], position, LENGTH)
    out_grad = (coeff[:, None] * logp_grad.astype(jnp.float32)).astype(jnp.bfloat16)
    query_blocks = to_rollouts(queries)
    grad_blocks = to_rollouts(out_grad)
    keys_split = to_rollouts(key_vectors).reshape(ALLROLL, LENGTH, KVH * HEAD)

    def one_rollout(triple):
        query_roll, grad_roll, keys_roll = triple

        def add_block(running, block_in):
            query_blk, grad_blk, block_at = block_in
            partial_value = block_values(query_blk, grad_blk, keys_roll, block_at * half)
            rounded = lax.optimization_barrier(partial_value.astype(jnp.bfloat16))
            return (running + rounded.astype(jnp.float32), None)
        start_sum = jnp.zeros((LENGTH, KVH * HEAD), jnp.float32)
        running, _ = lax.scan(add_block, start_sum, (query_roll, grad_roll, jnp.arange(N_FSDP, dtype=jnp.int32)))
        return running.astype(jnp.bfloat16)
    rolled = lax.map(one_rollout, (query_blocks, grad_blocks, keys_split))
    values_grad = rolled.reshape(N_SIDE, ROLLS, N_FSDP, half, KVH * HEAD).transpose(0, 2, 1, 3, 4).reshape(ALLTOK, KVH * HEAD)
    input_grad = jnp.dot(values_grad, value_proj.T, preferred_element_type=jnp.float32).astype(jnp.bfloat16)
    weight_grad = jnp.dot(attn_inputs.T, values_grad, preferred_element_type=jnp.float32)
    new_proj, new_first, new_second = adam_rows(value_proj, weight_grad, first_moment, second_moment)
    return (input_grad, new_proj, new_first, new_second)
```

```python
import functools
import math

import jax
import jax.numpy as jnp
from jax import lax
from jax.experimental import pallas as pl
from jax.experimental.pallas import tpu as pltpu
from jax.sharding import Mesh
from jax.sharding import PartitionSpec as P

QH = 20
KVH = 4
HEAD = 128
ROLLS = 2
PAIR = 2


clip_low = 0.8
clip_high = 1.2
decay_first = 0.9
decay_second = 0.95
step_rate = 0.001
weight_decay = 0.1
adam_eps = 1e-08
bias_first = 1.0 - 0.9**10
bias_second = 1.0 - 0.95**10


def advantages(rewards, group_ids):
    same = (group_ids[:, None] == group_ids[None, :]).astype(jnp.float32)
    counts = jnp.sum(same, axis=1)
    own_mean = jnp.sum(same * rewards[None, :], axis=1) / counts
    spread = rewards - own_mean
    variance = jnp.sum(same * (spread * spread)[None, :], axis=1) / counts
    return spread / jnp.maximum(jnp.sqrt(variance), 1.0)


def coefficient(new_lp, old_lp, adv_tok, len_tok, pos_tok, full_len):
    ratio_now = jnp.exp(new_lp - old_lp)
    clipped = jnp.clip(ratio_now, clip_low, clip_high)
    active = (ratio_now * adv_tok <= clipped * adv_tok) & (pos_tok < len_tok)
    len_weight = full_len / len_tok.astype(jnp.float32)
    return jnp.where(active, -adv_tok * ratio_now * len_weight, 0.0)


def attention_kernel(slots, half, place, q_own, q_far, g_own, g_far, *refs):
    key_refs, part_refs, probs = refs[:slots], refs[slots : 2 * slots], refs[2 * slots]
    z_index, x_index = place[0], place[1]
    per_group = q_own.shape[1] // HEAD
    block = PAIR * half
    scale = 1.0 / math.sqrt(HEAD)

    def spot(dim):
        at = lax.broadcasted_iota(jnp.int32, (block, block), dim)
        return jnp.where(at < half, at + x_index * half, at - half + (1 - x_index) * half)

    causal = spot(0) <= spot(1)
    for roll in range(ROLLS):
        rows = slice(roll * half, (roll + 1) * half)
        far_rows = slice((ROLLS + roll) * half, (ROLLS + roll + 1) * half)
        keys = jnp.concatenate(
            [key_refs[n][part, :] for n in range(slots) for part in (rows, far_rows)], axis=0
        )
        grads = []
        for head in range(per_group):
            cols = slice(head * HEAD, (head + 1) * HEAD)
            query = jnp.concatenate([q_own[rows, cols], q_far[rows, cols]], axis=0)
            grads.append(jnp.concatenate([g_own[rows, cols], g_far[rows, cols]], axis=0))
            scores = (
                lax.dot_general(
                    keys, query, (((1,), (1,)), ((), ())), preferred_element_type=jnp.float32
                )
                * scale
            )
            pieces = [jnp.where(causal, scores[:block], -1e30)]
            for n in range(1, slots):
                pieces.append(
                    jnp.where(z_index >= n, scores[n * block : (n + 1) * block], -1e30)
                )
            top = functools.reduce(
                jnp.maximum, [jnp.max(piece, axis=0, keepdims=True) for piece in pieces]
            )
            expo = [jnp.exp(piece - top) for piece in pieces]
            total = sum(jnp.sum(piece, axis=0, keepdims=True) for piece in expo)
            inverse = 1.0 / total
            for n in range(slots):
                probs[n * block : (n + 1) * block, head * block : (head + 1) * block] = (
                    expo[n] * inverse
                ).astype(jnp.bfloat16)
        summed = jnp.dot(
            probs[...], jnp.concatenate(grads, axis=0), preferred_element_type=jnp.float32
        ).astype(jnp.bfloat16)
        for n in range(slots):
            part_refs[n][rows, :] = summed[n * block : n * block + half]
            part_refs[n][far_rows, :] = summed[n * block + half : (n + 1) * block]


def attention_parts(place, q_own, q_far, g_own, g_far, key_blocks):
    slots = len(key_blocks)
    tok_rows, q_cols = q_own.shape
    kv_heads = key_blocks[0].shape[1] // HEAD
    per_head = q_cols // kv_heads
    half = tok_rows // ROLLS
    q_spec = pl.BlockSpec((tok_rows, per_head), lambda h, place: (0, h))
    k_spec = pl.BlockSpec((PAIR * tok_rows, HEAD), lambda h, place: (0, h))
    shape = jax.ShapeDtypeStruct(key_blocks[0].shape, jnp.bfloat16)
    work = 4 * kv_heads * per_head * ROLLS * (PAIR * half) ** 2 * slots
    return pl.pallas_call(
        functools.partial(attention_kernel, slots, half),
        grid_spec=pltpu.PrefetchScalarGridSpec(
            num_scalar_prefetch=1,
            grid=(kv_heads,),
            in_specs=[q_spec] * 4 + [k_spec] * slots,
            out_specs=[k_spec] * slots,
            scratch_shapes=[
                pltpu.VMEM(
                    (slots * PAIR * half, per_head // HEAD * PAIR * half), jnp.bfloat16
                )
            ],
        ),
        out_shape=[shape] * slots,
        cost_estimate=pl.CostEstimate(
            flops=work, bytes_accessed=8 * tok_rows * q_cols, transcendentals=work // 256
        ),
    )(place, q_own, q_far, g_own, g_far, *key_blocks)


def adam_rows(old_rows, grad_rows, first_moment, second_moment):
    first = decay_first * first_moment.astype(jnp.float32) + (1.0 - decay_first) * grad_rows
    second = (
        decay_second * second_moment.astype(jnp.float32)
        + (1.0 - decay_second) * grad_rows * grad_rows
    )
    weight_now = old_rows.astype(jnp.float32)
    update = (
        first / bias_first / (jnp.sqrt(second / bias_second) + adam_eps) + weight_decay * weight_now
    )
    return (
        (weight_now - step_rate * update).astype(jnp.bfloat16),
        first.astype(jnp.bfloat16),
        second.astype(jnp.bfloat16),
    )


def shift(value, axis, step, wrap=True):
    size = lax.axis_size(axis)
    pairs = [(i, (i + step) % size) for i in range(size) if wrap or 0 <= i + step < size]
    return lax.ppermute(value, axis, pairs)


def ordered(received, index):
    size = len(received)
    if size == 2:
        flag = index == 0
        return jnp.stack(
            [
                jnp.where(flag, received[0], received[1]),
                jnp.where(flag, received[1], received[0]),
            ]
        )
    turned = jnp.stack([received[-k % size] for k in range(size)])
    return lax.dynamic_slice_in_dim(
        jnp.concatenate([turned, turned], axis=0), (size - index) % size, size, 0
    )


def gathered(value, axis):
    return ordered(
        [value] + [shift(value, axis, k) for k in range(1, lax.axis_size(axis))],
        lax.axis_index(axis),
    )


def exchanged(value, axis, dim):
    size = lax.axis_size(axis)
    index = lax.axis_index(axis)
    received = []
    for k in range(size):
        piece = lax.dynamic_index_in_dim(value, (index + k) % size, dim, keepdims=False)
        received.append(piece if k == 0 else shift(piece, axis, k))
    return ordered(received, index)


def shards(
    attn_inputs,
    queries,
    key_vectors,
    logp_grad,
    new_logp,
    old_logp,
    rewards,
    group_ids,
    lengths,
    value_proj,
    first_moment,
    second_moment,
):
    z_size, y_size, core_size = lax.axis_size("z"), lax.axis_size("y"), lax.axis_size("core")
    z_index, x_index = lax.axis_index("z"), lax.axis_index("x")
    side_size = y_size * core_size
    side_index = lax.axis_index("y") * core_size + lax.axis_index("core")
    tok_rows, depth = attn_inputs.shape
    half = tok_rows // ROLLS
    full_len = half * z_size * PAIR
    width = key_vectors.shape[1]
    shard_rows = first_moment.shape[0]
    first_row = x_index == 0

    def split(array):
        mid = array.shape[1] // 2
        low, high = array[:, :mid], array[:, mid:]
        return jnp.where(first_row, low, high), jnp.where(first_row, high, low)

    key_own, key_out = split(key_vectors)
    key_far = shift(key_out, "x", 1)
    q_own, q_out = split(queries)
    q_far = shift(q_out, "x", 1)

    advantage = advantages(rewards, group_ids)
    rolls = jnp.arange(rewards.shape[0], dtype=jnp.int32)[None, :]
    mine = rolls == side_index * ROLLS + jnp.arange(ROLLS, dtype=jnp.int32)[:, None]
    adv_roll = jnp.sum(jnp.where(mine, advantage[None, :], 0.0), axis=1)
    len_roll = jnp.sum(jnp.where(mine, lengths[None, :], 0), axis=1)
    position = (z_index * PAIR + x_index) * half + jnp.arange(half, dtype=jnp.int32)
    coeff = coefficient(
        new_logp.reshape(ROLLS, half),
        old_logp.reshape(ROLLS, half),
        adv_roll[:, None],
        len_roll[:, None],
        position[None, :],
        full_len,
    ).reshape(tok_rows)
    out_grad = (coeff[:, None] * logp_grad.astype(jnp.float32)).astype(jnp.bfloat16)
    g_own, g_out = split(out_grad)
    g_far = shift(g_out, "x", 1)

    key_block = jnp.concatenate([key_own, key_far], axis=0)
    key_blocks = [key_block] + [shift(key_block, "z", k, False) for k in range(1, z_size)]

    turned = attn_inputs.T.reshape(z_size, PAIR, y_size, core_size, shard_rows, tok_rows)
    by_y = exchanged(turned, "y", 2)
    by_core = exchanged(by_y, "core", 3)
    by_x = exchanged(by_core, "x", 3)
    in_columns = by_x.transpose(3, 4, 0, 2, 1, 5).reshape(
        z_size * shard_rows, PAIR * side_size * tok_rows
    )

    own_proj = lax.dynamic_slice_in_dim(value_proj, side_index * shard_rows, shard_rows, 0)
    proj_rows = gathered(own_proj, "z").reshape(z_size * shard_rows, width)

    place = jnp.stack([z_index, x_index]).astype(jnp.int32)
    parts = attention_parts(place, q_own, q_far, g_own, g_far, key_blocks)
    total = parts[0].astype(jnp.float32)
    for k in range(1, z_size):
        total = total + shift(parts[k], "z", -k, False).astype(jnp.float32)
    mine_cols = total.astype(jnp.bfloat16)
    far_cols = shift(mine_cols, "x", 1)

    def turn(array):
        return jnp.concatenate([array[tok_rows:], array[:tok_rows]], axis=0)

    pair_grad = jnp.where(
        first_row,
        jnp.concatenate([mine_cols, turn(far_cols)], axis=1),
        jnp.concatenate([far_cols, turn(mine_cols)], axis=1),
    ).reshape(PAIR, tok_rows, width)
    y_grad = gathered(pair_grad, "y")
    core_grad = gathered(y_grad, "core")
    values_grad = core_grad.transpose(2, 1, 0, 3, 4).reshape(-1, width)

    weight_grad = jnp.dot(
        in_columns, values_grad, preferred_element_type=jnp.float32
    ).reshape(z_size, shard_rows, width)
    shard_grad = lax.dynamic_index_in_dim(weight_grad, z_index, 0, keepdims=False)
    rounded = weight_grad.astype(jnp.bfloat16)
    for k in range(1, z_size):
        piece = lax.dynamic_index_in_dim(rounded, (z_index + k) % z_size, 0, keepdims=False)
        shard_grad = shard_grad + shift(piece, "z", k).astype(jnp.float32)

    grad_cols = lax.dot_general(
        proj_rows, values_grad, (((1,), (1,)), ((), ())), preferred_element_type=jnp.float32
    ).astype(jnp.bfloat16)
    grad_send = (
        grad_cols.reshape(z_size * shard_rows, PAIR * side_size, tok_rows)
        .transpose(1, 0, 2)
        .reshape(-1, tok_rows)
    )
    grad_back = lax.all_to_all(
        grad_send, ("x", "y", "core"), split_axis=0, concat_axis=0, tiled=True
    ).reshape(PAIR, side_size, z_size, shard_rows, tok_rows)
    input_grad = grad_back.transpose(4, 2, 0, 1, 3).reshape(tok_rows, depth)

    new_rows, new_first, new_second = adam_rows(own_proj, shard_grad, first_moment, second_moment)
    new_proj = lax.all_gather(new_rows, ("y", "core"), axis=0, tiled=True)
    return (input_grad, new_proj, new_first, new_second)


def solution(mesh):
    fsdp_size, side_size = mesh.shape["fsdp"], mesh.shape["side"]
    fine = Mesh(
        mesh.devices.reshape(fsdp_size // PAIR, PAIR, side_size // 2, 2),
        ("z", "x", "y", "core"),
    )
    tokens = ("y", "core", "z", "x")
    placed = (
        P(tokens, None),
        P(tokens, None),
        P(tokens, None),
        P(tokens, None),
        P(tokens),
        P(tokens),
        P(),
        P(),
        P(),
        P(("z", "x"), None),
        P(("z", "x", "y", "core"), None),
        P(("z", "x", "y", "core"), None),
    )
    return jax.shard_map(
        shards,
        mesh=fine,
        in_specs=placed,
        out_specs=(
            P(tokens, None),
            P(("z", "x"), None),
            P(("z", "x", "y", "core"), None),
            P(("z", "x", "y", "core"), None),
        ),
        check_vma=False,
    )
```

```python
import functools
import math

import jax
import jax.numpy as jnp
from jax import lax
from jax.experimental import pallas as pl
from jax.experimental.pallas import tpu as pltpu
from jax.sharding import Mesh
from jax.sharding import PartitionSpec as P


HEAD = 128
ROLLS = 2
PAIR = 2


clip_low = 0.8
clip_high = 1.2
decay_first = 0.9
decay_second = 0.95
step_rate = 0.001
weight_decay = 0.1
adam_eps = 1e-08
bias_first = 1.0 - 0.9**10
bias_second = 1.0 - 0.95**10


def advantages(rewards, group_ids):
    same = (group_ids[:, None] == group_ids[None, :]).astype(jnp.float32)
    counts = jnp.sum(same, axis=1)
    own_mean = jnp.sum(same * rewards[None, :], axis=1) / counts
    spread = rewards - own_mean
    variance = jnp.sum(same * (spread * spread)[None, :], axis=1) / counts
    return spread / jnp.maximum(jnp.sqrt(variance), 1.0)


def coefficient(new_lp, old_lp, adv_tok, len_tok, pos_tok, full_len):
    ratio_now = jnp.exp(new_lp - old_lp)
    clipped = jnp.clip(ratio_now, clip_low, clip_high)
    active = (ratio_now * adv_tok <= clipped * adv_tok) & (pos_tok < len_tok)
    len_weight = full_len / len_tok.astype(jnp.float32)
    return jnp.where(active, -adv_tok * ratio_now * len_weight, 0.0)


def attention_kernel(slots, half, place, q_own, q_far, g_own, g_far, c_own, c_far, *refs):
    key_refs, part_refs, probs = refs[:slots], refs[slots : 2 * slots], refs[2 * slots]
    z_index, x_index = place[0], place[1]
    per_group = q_own.shape[1] // HEAD
    block = PAIR * half
    scale = 1.0 / math.sqrt(HEAD)

    def spot(dim):
        at = lax.broadcasted_iota(jnp.int32, (block, block), dim)
        return jnp.where(at < half, at + x_index * half, at - half + (1 - x_index) * half)

    causal = spot(0) <= spot(1)
    for roll in range(ROLLS):
        rows = slice(roll * half, (roll + 1) * half)
        far_rows = slice((ROLLS + roll) * half, (ROLLS + roll + 1) * half)
        keys = jnp.concatenate(
            [key_refs[n][part, :] for n in range(slots) for part in (rows, far_rows)], axis=0
        )
        grads = []
        for head in range(per_group):
            cols = slice(head * HEAD, (head + 1) * HEAD)
            query = jnp.concatenate([q_own[rows, cols], q_far[rows, cols]], axis=0)
            grads += [
                (c[rows, :] * g[rows, cols].astype(jnp.float32)).astype(jnp.bfloat16)
                for c, g in ((c_own, g_own), (c_far, g_far))
            ]
            scores = (
                lax.dot_general(
                    keys, query, (((1,), (1,)), ((), ())), preferred_element_type=jnp.float32
                )
                * scale
            )
            pieces = [jnp.where(causal, scores[:block], -1e30)]
            for n in range(1, slots):
                pieces.append(
                    jnp.where(z_index >= n, scores[n * block : (n + 1) * block], -1e30)
                )
            top = functools.reduce(
                jnp.maximum, [jnp.max(piece, axis=0, keepdims=True) for piece in pieces]
            )
            expo = [jnp.exp(piece - top) for piece in pieces]
            total = sum(jnp.sum(piece, axis=0, keepdims=True) for piece in expo)
            inverse = 1.0 / total
            for n in range(slots):
                probs[n * block : (n + 1) * block, head * block : (head + 1) * block] = (
                    expo[n] * inverse
                ).astype(jnp.bfloat16)
        summed = jnp.dot(
            probs[...], jnp.concatenate(grads, axis=0), preferred_element_type=jnp.float32
        ).astype(jnp.bfloat16)
        for n in range(slots):
            part_refs[n][rows, :] = summed[n * block : n * block + half]
            part_refs[n][far_rows, :] = summed[n * block + half : (n + 1) * block]


def attention_parts(place, queries, q_far, logp_grad, g_far, c_own, c_far, key_blocks):
    slots = len(key_blocks)
    tok_rows, q_cols = q_far.shape
    kv_heads = key_blocks[0].shape[1] // HEAD
    per_head = q_cols // kv_heads
    half = tok_rows // ROLLS
    own_spec = pl.BlockSpec((tok_rows, per_head), lambda h, place: (0, place[1] * kv_heads + h))
    far_spec = pl.BlockSpec((tok_rows, per_head), lambda h, place: (0, h))
    coeff_spec = pl.BlockSpec((tok_rows, 1), lambda h, place: (0, 0))
    k_spec = pl.BlockSpec((PAIR * tok_rows, HEAD), lambda h, place: (0, h))
    shape = jax.ShapeDtypeStruct(key_blocks[0].shape, jnp.bfloat16)
    work = 4 * kv_heads * per_head * ROLLS * (PAIR * half) ** 2 * slots
    return pl.pallas_call(
        functools.partial(attention_kernel, slots, half),
        grid_spec=pltpu.PrefetchScalarGridSpec(
            num_scalar_prefetch=1,
            grid=(kv_heads,),
            in_specs=[own_spec, far_spec] * 2 + [coeff_spec] * 2 + [k_spec] * slots,
            out_specs=[k_spec] * slots,
            scratch_shapes=[
                pltpu.VMEM(
                    (slots * PAIR * half, per_head // HEAD * PAIR * half), jnp.bfloat16
                )
            ],
        ),
        out_shape=[shape] * slots,
        cost_estimate=pl.CostEstimate(
            flops=work, bytes_accessed=8 * tok_rows * q_cols, transcendentals=work // 256
        ),
    )(place, queries, q_far, logp_grad, g_far, c_own, c_far, *key_blocks)


def pack_kernel(place, k_own, k_far, q_far, g_far, *outs):
    for source, out in zip((k_own, k_far, q_far, g_far), outs):
        out[...] = source[...]


def packed(place, key_vectors, queries, logp_grad):
    tok_rows = queries.shape[0]
    steps = key_vectors.shape[1] // HEAD // PAIR
    q_cols = queries.shape[1] // PAIR // steps

    def spec(cols, far):
        def where(h, place):
            x = 1 - place[1] if far else place[1]
            return 0, x * steps + h

        return pl.BlockSpec((tok_rows, cols), where)

    def half(cols):
        return jax.ShapeDtypeStruct((tok_rows, steps * cols), jnp.bfloat16)

    return pl.pallas_call(
        pack_kernel,
        grid_spec=pltpu.PrefetchScalarGridSpec(
            num_scalar_prefetch=1,
            grid=(steps,),
            in_specs=[spec(HEAD, False), spec(HEAD, True), spec(q_cols, True), spec(q_cols, True)],
            out_specs=[
                pl.BlockSpec((tok_rows, cols), lambda h, place: (0, h))
                for cols in (HEAD, HEAD, q_cols, q_cols)
            ],
        ),
        out_shape=[half(HEAD), half(HEAD), half(q_cols), half(q_cols)],
        cost_estimate=pl.CostEstimate(
            flops=0, bytes_accessed=8 * tok_rows * steps * q_cols, transcendentals=0
        ),
    )(place, key_vectors, key_vectors, queries, logp_grad)


def owner_kernel(z_size, pieces, place, near, far, *refs):
    values, outs = refs[: 2 * pieces], refs[2 * pieces :]
    sources = [(c, y) for c in range(near.shape[0]) for y in range(near.shape[1])]
    first = jnp.concatenate([ref[...] for ref in values[:pieces]], axis=0)
    second = jnp.concatenate([ref[...] for ref in values[pieces:]], axis=0)
    half = first.shape[1]
    for k in range(z_size):
        owner = place[0] + k
        owner = jnp.where(owner >= z_size, owner - z_size, owner)
        near_cols = [near[c, y, owner] for c, y in sources]
        far_cols = [far[c, y, owner] for c, y in sources]
        own_first = [cols for pair in zip(near_cols, far_cols) for cols in pair]
        far_first = [cols for pair in zip(far_cols, near_cols) for cols in pair]
        outs[k][:, :half] = jnp.dot(
            jnp.concatenate(own_first, axis=1), first, preferred_element_type=jnp.float32
        ).astype(jnp.bfloat16)
        outs[k][:, half:] = jnp.dot(
            jnp.concatenate(far_first, axis=1), second, preferred_element_type=jnp.float32
        ).astype(jnp.bfloat16)


def owner_products(place, near, far, first, second):
    _, _, z_size, rows, _ = near.shape
    pieces = len(first)
    width = 2 * first[0].shape[1]
    shape = jax.ShapeDtypeStruct((rows, width), jnp.bfloat16)
    whole = pl.BlockSpec(memory_space=pltpu.VMEM)
    return pl.pallas_call(
        functools.partial(owner_kernel, z_size, pieces),
        in_specs=[pl.BlockSpec(memory_space=pltpu.SMEM)] + [whole] * (2 + 2 * pieces),
        out_specs=[whole] * z_size,
        out_shape=[shape] * z_size,
        cost_estimate=pl.CostEstimate(
            flops=4 * near.size * width, bytes_accessed=8 * near.size, transcendentals=0
        ),
    )(place, near, far, *first, *second)


def row_kernel(z_size, y_size, place, *refs):
    ends = 2 * y_size, len(refs) - 1 - 2 * y_size
    values, proj, outs = refs[: ends[0]], refs[ends[0] : ends[1]], refs[ends[1] : -1]
    rows_all = refs[-1]
    rows, tok_rows = proj[0].shape[1], outs[0].shape[0]
    for c, ref in enumerate(proj):
        at_core = place[3] - c
        at_core = jnp.where(at_core < 0, at_core + len(proj), at_core)
        for k in range(z_size):
            at_z = place[0] - k
            at_z = jnp.where(at_z < 0, at_z + z_size, at_z)
            start = pl.multiple_of((at_z * len(proj) + at_core) * rows, rows)
            rows_all[pl.ds(start, rows), :] = ref[k]
    for y in range(y_size):
        first, second = values[y], values[y_size + y]
        own = [first[:tok_rows, :], second[tok_rows:, :]]
        far = [first[tok_rows:, :], second[:tok_rows, :]]
        for x, (low, high) in enumerate((own, far)):
            tokens = jnp.where(
                place[1] == 0,
                jnp.concatenate([low, high], axis=1),
                jnp.concatenate([high, low], axis=1),
            )
            outs[x * y_size + y][...] = lax.dot_general(
                tokens,
                rows_all[...],
                (((1,), (1,)), ((), ())),
                preferred_element_type=jnp.float32,
            ).astype(jnp.bfloat16)


def by_place(blocks, index):
    size = len(blocks)
    back = jnp.stack([blocks[-k % size] for k in range(size)])
    start = jnp.where(index == 0, 0, size - index)
    return lax.dynamic_slice_in_dim(jnp.concatenate([back, back], axis=0), start, size, 0)


def plain_row_products(place, first, second, proj):
    z_size, _, width = proj[0].shape
    tok_rows = first[0].shape[0] // PAIR
    cores = by_place(proj, place[3])
    along = by_place([cores[:, k] for k in range(z_size)], place[0])
    every = along.reshape(-1, width)
    outs = []
    for x in range(PAIR):
        for low, high in zip(first, second):
            near, far = slice(0, tok_rows), slice(tok_rows, PAIR * tok_rows)
            low, high = (low[near], high[far]) if x == 0 else (low[far], high[near])
            tokens = jnp.where(
                place[1] == 0,
                jnp.concatenate([low, high], axis=1),
                jnp.concatenate([high, low], axis=1),
            )
            outs.append(
                jnp.dot(tokens, every.T, preferred_element_type=jnp.float32).astype(jnp.bfloat16)
            )
    return outs


def row_products(place, first, second, proj):
    z_size, rows, width = proj[0].shape
    y_size = len(first)
    tok_rows = first[0].shape[0] // PAIR
    cols = z_size * len(proj) * rows
    if rows % 16 or cols % 128:
        return plain_row_products(place, first, second, proj)
    whole = pl.BlockSpec(memory_space=pltpu.VMEM)
    shape = jax.ShapeDtypeStruct((tok_rows, cols), jnp.bfloat16)
    return pl.pallas_call(
        functools.partial(row_kernel, z_size, y_size),
        in_specs=[pl.BlockSpec(memory_space=pltpu.SMEM)] + [whole] * (2 * y_size + len(proj)),
        out_specs=[whole] * (2 * y_size),
        out_shape=[shape] * (2 * y_size),
        scratch_shapes=[pltpu.VMEM((cols, width), jnp.bfloat16)],
        cost_estimate=pl.CostEstimate(
            flops=4 * y_size * tok_rows * width * cols,
            bytes_accessed=2 * cols * (width + 2 * y_size * tok_rows),
            transcendentals=0,
        ),
    )(place, *first, *second, *proj)


def final_kernel(z_size, place, *refs):
    pieces, out = refs[:-1], refs[-1]
    cols = pieces[0].shape[1] // z_size
    flags = place[1] == 0, place[2] == 0
    for z in range(z_size):
        part = slice(z * cols, (z + 1) * cols)
        near = [jnp.where(flags[1], pieces[y][:, part], pieces[1 - y][:, part]) for y in (0, 1)]
        far = [
            jnp.where(flags[1], pieces[2 + y][:, part], pieces[3 - y][:, part]) for y in (0, 1)
        ]
        near, far = jnp.concatenate(near, axis=1), jnp.concatenate(far, axis=1)
        wide = 2 * cols
        out[:, 2 * z * wide : (2 * z + 1) * wide] = jnp.where(flags[0], near, far)
        out[:, (2 * z + 1) * wide : (2 * z + 2) * wide] = jnp.where(flags[0], far, near)


def assembled(place, pieces, z_size):
    tokens = pieces[0].shape[0]
    y_size = len(pieces) // PAIR
    cols = pieces[0].shape[1] // z_size
    if y_size != 2 or 2 * cols % 128:
        split = [piece.reshape(tokens, z_size, cols) for piece in pieces]
        both = []
        for x in range(PAIR):
            found = jnp.stack(split[x * y_size : (x + 1) * y_size])
            start = jnp.where(place[2] == 0, 0, y_size - place[2])
            both.append(
                lax.dynamic_slice_in_dim(
                    jnp.concatenate([found, found], axis=0), start, y_size, 0
                )
            )
        both = jnp.stack(both)
        both = jnp.where(place[1] == 0, both, both[::-1])
        return both.transpose(2, 3, 0, 1, 4).reshape(tokens, -1)
    whole = pl.BlockSpec(memory_space=pltpu.VMEM)
    return pl.pallas_call(
        functools.partial(final_kernel, z_size),
        in_specs=[pl.BlockSpec(memory_space=pltpu.SMEM)] + [whole] * len(pieces),
        out_specs=whole,
        out_shape=jax.ShapeDtypeStruct((tokens, len(pieces) * z_size * cols), jnp.bfloat16),
        cost_estimate=pl.CostEstimate(
            flops=0, bytes_accessed=4 * tokens * len(pieces) * z_size * cols, transcendentals=0
        ),
    )(place, *pieces)


def adam_rows(old_rows, grad_rows, first_moment, second_moment):
    first = decay_first * first_moment.astype(jnp.float32) + (1.0 - decay_first) * grad_rows
    second = (
        decay_second * second_moment.astype(jnp.float32)
        + (1.0 - decay_second) * grad_rows * grad_rows
    )
    weight_now = old_rows.astype(jnp.float32)
    update = (
        first / bias_first / (jnp.sqrt(second / bias_second) + adam_eps) + weight_decay * weight_now
    )
    return (
        (weight_now - step_rate * update).astype(jnp.bfloat16),
        first.astype(jnp.bfloat16),
        second.astype(jnp.bfloat16),
    )


def shift(value, axis, step, wrap=True):
    size = lax.axis_size(axis)
    pairs = [(i, (i + step) % size) for i in range(size) if wrap or 0 <= i + step < size]
    return lax.ppermute(value, axis, pairs)


def turned(index, step, size):
    moved = index + step
    return jnp.where(moved >= size, moved - size, moved)


def cut(value, index, dim):
    return lax.dynamic_index_in_dim(value, index, dim, keepdims=False)


def step(
    attn_inputs,
    queries,
    key_vectors,
    logp_grad,
    new_logp,
    old_logp,
    rewards,
    group_ids,
    lengths,
    value_proj,
    first_moment,
    second_moment,
):
    z_size, y_size, core_size = lax.axis_size("z"), lax.axis_size("y"), lax.axis_size("core")
    z_index, x_index = lax.axis_index("z"), lax.axis_index("x")
    side_index = lax.axis_index("y") * core_size + lax.axis_index("core")
    tok_rows, _ = attn_inputs.shape
    half = tok_rows // ROLLS
    full_len = half * z_size * PAIR
    width = key_vectors.shape[1]
    shard_rows = first_moment.shape[0]
    y_index, core_index = lax.axis_index("y"), lax.axis_index("core")
    place = jnp.stack([z_index, x_index, y_index, core_index]).astype(jnp.int32)

    key_own, key_out, q_out, g_out = packed(place, key_vectors, queries, logp_grad)
    key_far = shift(key_out, "x", 1)
    q_far = shift(q_out, "x", 1)
    g_far = shift(g_out, "x", 1)
    key_block = jnp.concatenate([key_own, key_far], axis=0)
    key_blocks = [key_block] + [shift(key_block, "z", k, False) for k in range(1, z_size)]

    columns = attn_inputs.T.reshape(z_size, PAIR, y_size, core_size, shard_rows, tok_rows)
    by_y = [cut(columns, y_index, 2)] + [
        shift(cut(columns, turned(y_index, k, y_size), 2), "y", k)
        for k in range(1, y_size)
    ]
    by_core = [
        jnp.stack([cut(block, core_index, 2) for block in by_y]),
        shift(jnp.stack([cut(block, 1 - core_index, 2) for block in by_y]), "core", 1),
    ]
    near_cols = jnp.stack([cut(block, x_index, 2) for block in by_core])
    far_cols = shift(jnp.stack([cut(block, 1 - x_index, 2) for block in by_core]), "x", 1)

    advantage = advantages(rewards, group_ids)
    rolls = jnp.arange(rewards.shape[0], dtype=jnp.int32)[None, :]
    mine = rolls == side_index * ROLLS + jnp.arange(ROLLS, dtype=jnp.int32)[:, None]
    adv_roll = jnp.sum(jnp.where(mine, advantage[None, :], 0.0), axis=1)
    len_roll = jnp.sum(jnp.where(mine, lengths[None, :], 0), axis=1)
    position = (z_index * PAIR + x_index) * half + jnp.arange(half, dtype=jnp.int32)
    coeff = coefficient(
        new_logp.reshape(ROLLS, half),
        old_logp.reshape(ROLLS, half),
        adv_roll[:, None],
        len_roll[:, None],
        position[None, :],
        full_len,
    ).reshape(tok_rows)
    coeff_far = shift(coeff, "x", 1)

    own_proj = lax.dynamic_slice_in_dim(value_proj, side_index * shard_rows, shard_rows, 0)
    own_proj = lax.optimization_barrier(own_proj)
    own_rows = jnp.stack([own_proj] + [shift(own_proj, "z", k) for k in range(1, z_size)])
    proj = [own_rows, shift(own_rows, "core", 1)]

    parts = attention_parts(
        place,
        queries,
        q_far,
        logp_grad,
        g_far,
        coeff.reshape(tok_rows, 1),
        coeff_far.reshape(tok_rows, 1),
        key_blocks,
    )
    total = parts[0].astype(jnp.float32)
    for k in range(1, z_size):
        arrived = shift(parts[k], "z", -k, False)
        total = total + arrived.astype(jnp.float32)

    def over_sides(value):
        found = [value] + [shift(value, "y", k) for k in range(1, y_size)]
        return found + [shift(block, "core", 1) for block in found]

    first_cols = total.astype(jnp.bfloat16)
    second_cols = shift(first_cols, "x", 1)
    first_all = over_sides(first_cols)
    second_all = over_sides(second_cols)

    pieces = owner_products(place, near_cols, far_cols, first_all, second_all)
    arrived = [shift(pieces[k], "z", k) for k in range(1, z_size)]
    shard_grad = pieces[0].astype(jnp.float32)
    for piece in arrived:
        shard_grad = shard_grad + piece.astype(jnp.float32)

    products = row_products(place, first_all[:y_size], second_all[:y_size], proj)
    found = list(products)
    for k in range(1, y_size):
        found[k] = shift(products[k], "y", -k)
    found[y_size] = shift(products[y_size], "x", 1)
    for k in range(1, y_size):
        pairs = [
            (x * y_size + y, (1 - x) * y_size + (y - k) % y_size)
            for x in range(PAIR)
            for y in range(y_size)
        ]
        found[y_size + k] = lax.ppermute(products[y_size + k], ("x", "y"), pairs)
    input_grad = assembled(place, found, z_size)

    swap = jnp.concatenate([shard_grad[:, width // 2 :], shard_grad[:, : width // 2]], axis=1)
    new_rows, new_first, new_second = adam_rows(
        own_proj, jnp.where(x_index == 0, shard_grad, swap), first_moment, second_moment
    )
    new_proj = lax.all_gather(new_rows, ("y", "core"), axis=0, tiled=True)
    return (input_grad, new_proj, new_first, new_second)


def solution(mesh):
    fsdp_size, side_size = mesh.shape["fsdp"], mesh.shape["side"]
    fine = Mesh(
        mesh.devices.reshape(fsdp_size // PAIR, PAIR, side_size // 2, 2),
        ("z", "x", "y", "core"),
    )
    tokens = ("y", "core", "z", "x")
    placed = (
        P(tokens, None),
        P(tokens, None),
        P(tokens, None),
        P(tokens, None),
        P(tokens),
        P(tokens),
        P(),
        P(),
        P(),
        P(("z", "x"), None),
        P(("z", "x", "y", "core"), None),
        P(("z", "x", "y", "core"), None),
    )
    return jax.shard_map(
        step,
        mesh=fine,
        in_specs=placed,
        out_specs=(
            P(tokens, None),
            P(("z", "x"), None),
            P(("z", "x", "y", "core"), None),
            P(("z", "x", "y", "core"), None),
        ),
        check_vma=False,
    )
```

```python
import functools
import math

import jax
import jax.numpy as jnp
from jax import lax
from jax.experimental import pallas as pl
from jax.experimental.pallas import tpu as pltpu
from jax.sharding import Mesh
from jax.sharding import PartitionSpec as P


HEAD = 128
ROLLS = 2
PAIR = 2


clip_low = 0.8
clip_high = 1.2
decay_first = 0.9
decay_second = 0.95
step_rate = 0.001
weight_decay = 0.1
adam_eps = 1e-08
bias_first = 1.0 - 0.9**10
bias_second = 1.0 - 0.95**10

ROOM = pltpu.CompilerParams(vmem_limit_bytes=16 * 2**20)


def advantages(rewards, group_ids):
    same = (group_ids[:, None] == group_ids[None, :]).astype(jnp.float32)
    counts = jnp.sum(same, axis=1)
    own_mean = jnp.sum(same * rewards[None, :], axis=1) / counts
    spread = rewards - own_mean
    variance = jnp.sum(same * (spread * spread)[None, :], axis=1) / counts
    return spread / jnp.maximum(jnp.sqrt(variance), 1.0)


def coefficient(new_lp, old_lp, adv_tok, len_tok, pos_tok, full_len):
    ratio_now = jnp.exp(new_lp - old_lp)
    clipped = jnp.clip(ratio_now, clip_low, clip_high)
    active = (ratio_now * adv_tok <= clipped * adv_tok) & (pos_tok < len_tok)
    len_weight = full_len / len_tok.astype(jnp.float32)
    return jnp.where(active, -adv_tok * ratio_now * len_weight, 0.0)


def attention_kernel(slots, half, place, q_own, q_far, g_own, g_far, c_own, c_far, *refs):
    key_refs, part_refs, probs = refs[:slots], refs[slots : 2 * slots], refs[2 * slots]
    z_index, x_index = place[0], place[1]
    per_group = q_own.shape[1] // HEAD
    block = PAIR * half
    scale = 1.0 / math.sqrt(HEAD)

    def spot(dim):
        at = lax.broadcasted_iota(jnp.int32, (block, block), dim)
        return jnp.where(at < half, at + x_index * half, at - half + (1 - x_index) * half)

    causal = spot(0) <= spot(1)
    for roll in range(ROLLS):
        rows = slice(roll * half, (roll + 1) * half)
        far_rows = slice((ROLLS + roll) * half, (ROLLS + roll + 1) * half)
        keys = jnp.concatenate(
            [key_refs[n][part, :] for n in range(slots) for part in (rows, far_rows)], axis=0
        )
        grads = []
        coeff = jnp.concatenate([c_own[roll : roll + 1, :], c_far[roll : roll + 1, :]], axis=1)
        for head in range(per_group):
            cols = slice(head * HEAD, (head + 1) * HEAD)
            query = jnp.concatenate([q_own[rows, cols], q_far[rows, cols]], axis=0)
            grads += [g_own[rows, cols], g_far[rows, cols]]
            scores = (
                lax.dot_general(
                    keys, query, (((1,), (1,)), ((), ())), preferred_element_type=jnp.float32
                )
                * scale
            )
            pieces = [jnp.where(causal, scores[:block], -1e30)]
            for n in range(1, slots):
                pieces.append(
                    jnp.where(z_index >= n, scores[n * block : (n + 1) * block], -1e30)
                )
            top = functools.reduce(
                jnp.maximum, [jnp.max(piece, axis=0, keepdims=True) for piece in pieces]
            )
            expo = [jnp.exp(piece - top) for piece in pieces]
            total = sum(jnp.sum(piece, axis=0, keepdims=True) for piece in expo)
            weight = coeff / total
            for n in range(slots):
                probs[n * block : (n + 1) * block, head * block : (head + 1) * block] = (
                    expo[n] * weight
                ).astype(jnp.bfloat16)
        summed = jnp.dot(
            probs[...], jnp.concatenate(grads, axis=0), preferred_element_type=jnp.float32
        ).astype(jnp.bfloat16)
        for n in range(slots):
            part_refs[n][rows, :] = summed[n * block : n * block + half]
            part_refs[n][far_rows, :] = summed[n * block + half : (n + 1) * block]


def attention_parts(place, queries, q_far, logp_grad, g_far, c_own, c_far, key_blocks):
    slots = len(key_blocks)
    tok_rows, q_cols = q_far.shape
    kv_heads = key_blocks[0].shape[1] // HEAD
    per_head = q_cols // kv_heads
    half = tok_rows // ROLLS
    own_spec = pl.BlockSpec((tok_rows, per_head), lambda h, place: (0, place[1] * kv_heads + h))
    far_spec = pl.BlockSpec((tok_rows, per_head), lambda h, place: (0, h))
    coeff_spec = pl.BlockSpec(c_own.shape, lambda h, place: (0, 0))
    k_spec = pl.BlockSpec((PAIR * tok_rows, HEAD), lambda h, place: (0, h))
    shape = jax.ShapeDtypeStruct(key_blocks[0].shape, jnp.bfloat16)
    work = 4 * kv_heads * per_head * ROLLS * (PAIR * half) ** 2 * slots
    return pl.pallas_call(
        functools.partial(attention_kernel, slots, half),
        grid_spec=pltpu.PrefetchScalarGridSpec(
            num_scalar_prefetch=1,
            grid=(kv_heads,),
            in_specs=[own_spec, far_spec] * 2 + [coeff_spec] * 2 + [k_spec] * slots,
            out_specs=[k_spec] * slots,
            scratch_shapes=[
                pltpu.VMEM(
                    (slots * PAIR * half, per_head // HEAD * PAIR * half), jnp.bfloat16
                )
            ],
        ),
        out_shape=[shape] * slots,
        compiler_params=ROOM,
        cost_estimate=pl.CostEstimate(
            flops=work, bytes_accessed=8 * tok_rows * q_cols, transcendentals=work // 256
        ),
    )(place, queries, q_far, logp_grad, g_far, c_own, c_far, *key_blocks)


def pack_kernel(place, k_own, k_far, q_far, g_far, *outs):
    for source, out in zip((k_own, k_far, q_far, g_far), outs):
        out[...] = source[...]


def packed(place, key_vectors, queries, logp_grad):
    tok_rows = queries.shape[0]
    steps = key_vectors.shape[1] // HEAD // PAIR
    q_cols = queries.shape[1] // PAIR // steps

    def spec(cols, far):
        def where(h, place):
            x = 1 - place[1] if far else place[1]
            return 0, x * steps + h

        return pl.BlockSpec((tok_rows, cols), where)

    def half(cols):
        return jax.ShapeDtypeStruct((tok_rows, steps * cols), jnp.bfloat16)

    return pl.pallas_call(
        pack_kernel,
        grid_spec=pltpu.PrefetchScalarGridSpec(
            num_scalar_prefetch=1,
            grid=(steps,),
            in_specs=[spec(HEAD, False), spec(HEAD, True), spec(q_cols, True), spec(q_cols, True)],
            out_specs=[
                pl.BlockSpec((tok_rows, cols), lambda h, place: (0, h))
                for cols in (HEAD, HEAD, q_cols, q_cols)
            ],
        ),
        out_shape=[
            jax.ShapeDtypeStruct((PAIR * tok_rows, steps * HEAD), jnp.bfloat16),
            half(HEAD),
            half(q_cols),
            half(q_cols),
        ],
        cost_estimate=pl.CostEstimate(
            flops=0, bytes_accessed=8 * tok_rows * steps * q_cols, transcendentals=0
        ),
    )(place, key_vectors, key_vectors, queries, logp_grad)


def owner_kernel(pieces, z_size, place, near, far, *refs):
    values, outs = refs[: 2 * pieces], refs[2 * pieces : 2 * pieces + z_size]
    token_rows = refs[2 * pieces + z_size]
    buffers, totals, sems = refs[-3:]
    copies = [
        pltpu.make_async_copy(source, buffers.at[n], sems.at[n])
        for n, source in enumerate((near, far))
    ]
    for copy in copies:
        copy.start()
    sides = near.shape[0] // PAIR
    rows, tokens = near.shape[2:]
    half = values[0].shape[1]
    for n, copy in enumerate(copies):
        copy.wait()
        for m in range(PAIR):
            columns = jnp.concatenate(
                [
                    buffers[n, (x + m) % PAIR * sides + y].reshape(z_size * rows, tokens)
                    for y in range(sides)
                    for x in range(PAIR)
                ],
                axis=1,
            )
            blocks = values[m * pieces + n * sides : m * pieces + (n + 1) * sides]
            product = jnp.dot(
                columns,
                jnp.concatenate([ref[...] for ref in blocks], axis=0),
                preferred_element_type=jnp.float32,
            )
            part = slice(m * half, (m + 1) * half)
            totals[:, part] = product if n == 0 else totals[:, part] + product
    flag = place[1] == 0
    for x in range(PAIR):
        for y in range(sides):
            low = values[y][x * tokens : (x + 1) * tokens, :]
            high = values[pieces + y][(1 - x) * tokens : (2 - x) * tokens, :]
            at = (x * sides + y) * tokens
            token_rows[at : at + tokens, :half] = jnp.where(flag, low, high)
            token_rows[at : at + tokens, half:] = jnp.where(flag, high, low)
    for k, out in enumerate(outs):
        at = place[0] + k
        start = pl.multiple_of(jnp.where(at >= z_size, at - z_size, at) * rows, rows)
        out[...] = totals[pl.ds(start, rows), :].astype(jnp.bfloat16)


def plain_owner_products(place, near, far, first, second):
    z_size, rows, tokens = near.shape[1:]
    sides = near.shape[0] // PAIR
    halves = []
    for m, blocks in enumerate((first, second)):
        total = 0.0
        for n, array in enumerate((near, far)):
            order = [(x + m) % PAIR * sides + y for y in range(sides) for x in range(PAIR)]
            columns = jnp.stack([array[at] for at in order], axis=2)
            total = total + jnp.dot(
                columns.reshape(z_size * rows, -1),
                jnp.concatenate(blocks[n * sides : (n + 1) * sides], axis=0),
                preferred_element_type=jnp.float32,
            )
        halves.append(total.astype(jnp.bfloat16))
    every = jnp.concatenate(halves, axis=1).reshape(z_size, rows, -1)
    groups = []
    for x in range(PAIR):
        for y in range(sides):
            low = first[y][x * tokens : (x + 1) * tokens]
            high = second[y][(1 - x) * tokens : (2 - x) * tokens]
            groups.append(
                jnp.where(
                    place[1] == 0,
                    jnp.concatenate([low, high], axis=1),
                    jnp.concatenate([high, low], axis=1),
                )
            )
    return [cut(every, turned(place[0], k, z_size), 0) for k in range(z_size)] + [
        jnp.concatenate(groups, axis=0)
    ]


def owner_products(place, near, far, first, second):
    z_size, rows, tokens = near.shape[1:]
    if rows % 16:
        return plain_owner_products(place, near, far, first, second)
    pieces = len(first)
    width = 2 * first[0].shape[1]
    whole = pl.BlockSpec(memory_space=pltpu.VMEM)
    shape = jax.ShapeDtypeStruct((rows, width), jnp.bfloat16)
    return pl.pallas_call(
        functools.partial(owner_kernel, pieces, z_size),
        in_specs=[pl.BlockSpec(memory_space=pltpu.SMEM)]
        + [pl.BlockSpec(memory_space=pl.ANY)] * 2
        + [whole] * (2 * pieces),
        out_specs=[whole] * (z_size + 1),
        out_shape=[shape] * z_size
        + [jax.ShapeDtypeStruct((near.shape[0] * tokens, width), jnp.bfloat16)],
        scratch_shapes=[
            pltpu.VMEM((2, *near.shape), jnp.bfloat16),
            pltpu.VMEM((z_size * rows, width), jnp.float32),
            pltpu.SemaphoreType.DMA((2,)),
        ],
        compiler_params=ROOM,
        cost_estimate=pl.CostEstimate(
            flops=4 * near.size * width, bytes_accessed=8 * near.size, transcendentals=0
        ),
    )(place, near, far, *first, *second)


def row_kernel(z_size, groups, place, token_rows, *refs):
    proj, outs = refs[:4], refs[4 : 4 + groups]
    rows_all, sems = refs[-2:]
    rows, tok_rows = proj[0].shape[1], outs[0].shape[0]
    copies = []
    for k, bits in enumerate(flips(z_size)):
        for c in range(2):
            at_core = place[3] if c == 0 else 1 - place[3]
            start = ((place[0] ^ bits) * 2 + at_core) * rows
            group, at = divmod(k, z_size // 2)
            copies.append(
                pltpu.make_async_copy(
                    proj[2 * c + group].at[at],
                    rows_all.at[pl.ds(pl.multiple_of(start, rows), rows), :],
                    sems.at[2 * k + c],
                )
            )
    for copy in copies:
        copy.start()
    for copy in copies:
        copy.wait()
    product = lax.dot_general(
        token_rows[...],
        rows_all[...],
        (((1,), (1,)), ((), ())),
        preferred_element_type=jnp.float32,
    ).astype(jnp.bfloat16)
    for n, out in enumerate(outs):
        out[...] = product[n * tok_rows : (n + 1) * tok_rows]


def plane_kernel(place, columns, *outs):
    y_size = columns.shape[2]
    for x in range(PAIR):
        for y in range(y_size):
            at_x, at_y = place[1] + x, place[2] + y
            at_x = jnp.where(at_x >= PAIR, at_x - PAIR, at_x)
            at_y = jnp.where(at_y >= y_size, at_y - y_size, at_y)
            out = outs[x * y_size + y]
            for z in range(columns.shape[0]):
                out[z] = columns[z, at_x, at_y]


def core_kernel(place, *refs):
    pieces, (near, far) = refs[:-2], refs[-2:]
    for n, piece in enumerate(pieces):
        for z in range(piece.shape[0]):
            near[n, z] = piece[z, place[3]]
            far[n, z] = piece[z, 1 - place[3]]


def sliced(kernel, place, arrays, shapes):
    whole = pl.BlockSpec(memory_space=pltpu.VMEM)
    return pl.pallas_call(
        kernel,
        in_specs=[pl.BlockSpec(memory_space=pltpu.SMEM)] + [whole] * len(arrays),
        out_specs=[whole] * len(shapes),
        out_shape=[jax.ShapeDtypeStruct(shape, jnp.bfloat16) for shape in shapes],
        compiler_params=ROOM,
        cost_estimate=pl.CostEstimate(
            flops=0,
            bytes_accessed=4 * sum(math.prod(shape) for shape in shapes),
            transcendentals=0,
        ),
    )(place, *arrays)


def by_place(blocks, index):
    size = len(blocks)
    back = jnp.stack([blocks[-k % size] for k in range(size)])
    start = jnp.where(index == 0, 0, size - index)
    return lax.dynamic_slice_in_dim(jnp.concatenate([back, back], axis=0), start, size, 0)


def plain_row_products(place, token_rows, groups, proj):
    width = proj[0].shape[2]
    z_size = 2 * proj[0].shape[0]
    cores = by_place(
        [jnp.concatenate(proj[2 * c : 2 * c + 2], axis=0) for c in range(2)], place[3]
    )
    order = {bits: k for k, bits in enumerate(flips(z_size))}
    along = jnp.stack([cores[:, order[k]] for k in range(z_size)])
    along = jnp.take(along, jnp.arange(z_size, dtype=jnp.int32) ^ place[0], axis=0)
    every = along.reshape(-1, width)
    product = jnp.dot(token_rows, every.T, preferred_element_type=jnp.float32)
    return jnp.split(product.astype(jnp.bfloat16), groups)


def row_products(place, token_rows, groups, proj):
    _, rows, width = proj[0].shape
    z_size = 2 * proj[0].shape[0]
    tok_rows = token_rows.shape[0] // groups
    cols = 2 * z_size * rows
    if rows % 16 or cols % 128:
        return plain_row_products(place, token_rows, groups, proj)
    whole = pl.BlockSpec(memory_space=pltpu.VMEM)
    shape = jax.ShapeDtypeStruct((tok_rows, cols), jnp.bfloat16)
    return pl.pallas_call(
        functools.partial(row_kernel, z_size, groups),
        in_specs=[pl.BlockSpec(memory_space=pltpu.SMEM), whole]
        + [pl.BlockSpec(memory_space=pl.ANY)] * len(proj),
        out_specs=[whole] * groups,
        out_shape=[shape] * groups,
        scratch_shapes=[
            pltpu.VMEM((cols, width), jnp.bfloat16),
            pltpu.SemaphoreType.DMA((2 * z_size,)),
        ],
        compiler_params=ROOM,
        cost_estimate=pl.CostEstimate(
            flops=2 * groups * tok_rows * width * cols,
            bytes_accessed=2 * cols * (width + groups * tok_rows),
            transcendentals=0,
        ),
    )(place, token_rows, *proj)


def final_kernel(z_size, place, *refs):
    pieces, out = refs[:-1], refs[-1]
    cols = pieces[0].shape[1] // z_size
    flags = place[1] == 0, place[2] == 0
    for z in range(z_size):
        part = slice(z * cols, (z + 1) * cols)
        near = [jnp.where(flags[1], pieces[y][:, part], pieces[1 - y][:, part]) for y in (0, 1)]
        far = [
            jnp.where(flags[1], pieces[2 + y][:, part], pieces[3 - y][:, part]) for y in (0, 1)
        ]
        near, far = jnp.concatenate(near, axis=1), jnp.concatenate(far, axis=1)
        wide = 2 * cols
        out[:, 2 * z * wide : (2 * z + 1) * wide] = jnp.where(flags[0], near, far)
        out[:, (2 * z + 1) * wide : (2 * z + 2) * wide] = jnp.where(flags[0], far, near)


def assembled(place, pieces, z_size):
    tokens = pieces[0].shape[0]
    y_size = len(pieces) // PAIR
    cols = pieces[0].shape[1] // z_size
    if y_size != 2 or 2 * cols % 128:
        split = [piece.reshape(tokens, z_size, cols) for piece in pieces]
        both = []
        for x in range(PAIR):
            found = jnp.stack(split[x * y_size : (x + 1) * y_size])
            start = jnp.where(place[2] == 0, 0, y_size - place[2])
            both.append(
                lax.dynamic_slice_in_dim(
                    jnp.concatenate([found, found], axis=0), start, y_size, 0
                )
            )
        both = jnp.stack(both)
        both = jnp.where(place[1] == 0, both, both[::-1])
        return both.transpose(2, 3, 0, 1, 4).reshape(tokens, -1)
    steps = 2 if tokens % 64 == 0 else 1

    def rows(array_cols):
        return pl.BlockSpec((tokens // steps, array_cols), lambda i, place: (i, 0))

    return pl.pallas_call(
        functools.partial(final_kernel, z_size),
        grid_spec=pltpu.PrefetchScalarGridSpec(
            num_scalar_prefetch=1,
            grid=(steps,),
            in_specs=[rows(z_size * cols)] * len(pieces),
            out_specs=rows(len(pieces) * z_size * cols),
        ),
        out_shape=jax.ShapeDtypeStruct((tokens, len(pieces) * z_size * cols), jnp.bfloat16),
        compiler_params=ROOM,
        cost_estimate=pl.CostEstimate(
            flops=0, bytes_accessed=4 * tokens * len(pieces) * z_size * cols, transcendentals=0
        ),
    )(place, *pieces)


def adam_rows(old_rows, grad_rows, first_moment, second_moment):
    first = decay_first * first_moment.astype(jnp.float32) + (1.0 - decay_first) * grad_rows
    second = (
        decay_second * second_moment.astype(jnp.float32)
        + (1.0 - decay_second) * grad_rows * grad_rows
    )
    weight_now = old_rows.astype(jnp.float32)
    update = (
        first / bias_first / (jnp.sqrt(second / bias_second) + adam_eps) + weight_decay * weight_now
    )
    return (
        (weight_now - step_rate * update).astype(jnp.bfloat16),
        first.astype(jnp.bfloat16),
        second.astype(jnp.bfloat16),
    )


def shift(value, axis, step, wrap=True):
    size = lax.axis_size(axis)
    pairs = [(i, (i + step) % size) for i in range(size) if wrap or 0 <= i + step < size]
    return lax.ppermute(value, axis, pairs)


def turned(index, step, size):
    moved = index + step
    return jnp.where(moved >= size, moved - size, moved)


def z_bits(z_size):
    assert z_size & (z_size - 1) == 0
    return [1 << n for n in range(z_size.bit_length() - 2, -1, -1)]


def flips(z_size):
    bits = z_bits(z_size)
    return [
        functools.reduce(int.__xor__, [bit for n, bit in enumerate(bits) if k >> n & 1], 0)
        for k in range(z_size)
    ]


def cut(value, index, dim):
    return lax.dynamic_index_in_dim(value, index, dim, keepdims=False)


def step(
    attn_inputs,
    queries,
    key_vectors,
    logp_grad,
    new_logp,
    old_logp,
    rewards,
    group_ids,
    lengths,
    value_proj,
    first_moment,
    second_moment,
):
    z_size, y_size, core_size = lax.axis_size("z"), lax.axis_size("y"), lax.axis_size("core")
    z_index, x_index = lax.axis_index("z"), lax.axis_index("x")
    side_index = lax.axis_index("y") * core_size + lax.axis_index("core")
    tok_rows, _ = attn_inputs.shape
    half = tok_rows // ROLLS
    full_len = half * z_size * PAIR
    width = key_vectors.shape[1]
    shard_rows = first_moment.shape[0]
    y_index, core_index = lax.axis_index("y"), lax.axis_index("core")
    place = jnp.stack([z_index, x_index, y_index, core_index]).astype(jnp.int32)

    key_room, key_out, q_out, g_out = packed(place, key_vectors, queries, logp_grad)
    key_far = shift(key_out, "x", 1)
    q_far = shift(q_out, "x", 1)
    g_far = shift(g_out, "x", 1)
    key_block = lax.dynamic_update_slice(key_room, key_far, (tok_rows, 0))
    key_blocks = [key_block] + [shift(key_block, "z", k, False) for k in range(1, z_size)]
    columns = attn_inputs.T.reshape(z_size, PAIR, y_size, core_size, shard_rows, tok_rows)
    found = []
    block = (z_size, core_size, shard_rows, tok_rows)
    cuts = sliced(plane_kernel, place, [columns], [block] * (PAIR * y_size))
    for x in range(PAIR):
        for k in range(y_size):
            piece = cuts[x * y_size + k]
            if x or k:
                pairs = [
                    (a * y_size + b, (a + x) % PAIR * y_size + (b + k) % y_size)
                    for a in range(PAIR)
                    for b in range(y_size)
                ]
                piece = lax.ppermute(piece, ("x", "y"), pairs)
            found.append(piece)
    every = (PAIR * y_size, z_size, shard_rows, tok_rows)
    near_cols, far_cols = sliced(core_kernel, place, found, [every] * 2)
    far_cols = shift(far_cols, "core", 1)

    advantage = advantages(rewards, group_ids)
    rolls = jnp.arange(rewards.shape[0], dtype=jnp.int32)[None, :]
    mine = rolls == side_index * ROLLS + jnp.arange(ROLLS, dtype=jnp.int32)[:, None]
    adv_roll = jnp.sum(jnp.where(mine, advantage[None, :], 0.0), axis=1)
    len_roll = jnp.sum(jnp.where(mine, lengths[None, :], 0), axis=1)
    position = (z_index * PAIR + x_index) * half + jnp.arange(half, dtype=jnp.int32)
    coeff = coefficient(
        new_logp.reshape(ROLLS, half),
        old_logp.reshape(ROLLS, half),
        adv_roll[:, None],
        len_roll[:, None],
        position[None, :],
        full_len,
    )
    coeff_far = shift(coeff, "x", 1)

    own_proj = lax.dynamic_slice_in_dim(value_proj, side_index * shard_rows, shard_rows, 0)
    own_proj = lax.optimization_barrier(own_proj)
    bits = z_bits(z_size)
    known = own_proj[None]
    for n, bit in enumerate(bits):
        pairs = [(i, i ^ bit) for i in range(z_size)]
        arrived = lax.ppermute(known, "z", pairs)
        if n < len(bits) - 1:
            known = jnp.concatenate([known, arrived], axis=0)
    proj = [known, arrived, shift(known, "core", 1), shift(arrived, "core", 1)]

    parts = attention_parts(place, queries, q_far, logp_grad, g_far, coeff, coeff_far, key_blocks)
    total = parts[0].astype(jnp.float32)
    for k in range(1, z_size):
        arrived = shift(parts[k], "z", -k, False)
        total = total + arrived.astype(jnp.float32)

    def over_sides(value):
        found = [value] + [shift(value, "y", k) for k in range(1, y_size)]
        return found + [shift(block, "core", 1) for block in found]

    first_cols = total.astype(jnp.bfloat16)
    second_cols = shift(first_cols, "x", 1)
    first_all = over_sides(first_cols)
    second_all = over_sides(second_cols)

    pieces = owner_products(place, near_cols, far_cols, first_all, second_all)
    arrived = [shift(pieces[k], "z", k) for k in range(1, z_size)]
    shard_grad = pieces[0].astype(jnp.float32)
    for piece in arrived:
        shard_grad = shard_grad + piece.astype(jnp.float32)

    products = row_products(place, pieces[z_size], PAIR * y_size, proj)
    back = list(products)
    for k in range(1, y_size):
        back[k] = shift(products[k], "y", -k)
    back[y_size] = shift(products[y_size], "x", 1)
    for k in range(1, y_size):
        pairs = [
            (x * y_size + y, (1 - x) * y_size + (y - k) % y_size)
            for x in range(PAIR)
            for y in range(y_size)
        ]
        back[y_size + k] = lax.ppermute(products[y_size + k], ("x", "y"), pairs)
    input_grad = assembled(place, back, z_size)

    swap = jnp.concatenate([shard_grad[:, width // 2 :], shard_grad[:, : width // 2]], axis=1)
    new_rows, new_first, new_second = adam_rows(
        own_proj, jnp.where(x_index == 0, shard_grad, swap), first_moment, second_moment
    )
    sides = [new_rows] + [shift(new_rows, "y", k) for k in range(1, y_size)]
    others = [shift(block, "core", 1) for block in sides]
    if y_size == 2:
        columns = [
            [jnp.where(y_index == 0, blocks[y], blocks[1 - y]) for y in range(2)]
            for blocks in (sides, others)
        ]
    else:
        columns = [list(by_place(blocks, y_index)) for blocks in (sides, others)]
    new_proj = jnp.concatenate(
        [
            jnp.where(core_index == c, columns[0][y], columns[1][y])
            for y in range(y_size)
            for c in range(core_size)
        ],
        axis=0,
    )
    return (input_grad, new_proj, new_first, new_second)


def solution(mesh):
    fsdp_size, side_size = mesh.shape["fsdp"], mesh.shape["side"]
    fine = Mesh(
        mesh.devices.reshape(fsdp_size // PAIR, PAIR, side_size // 2, 2),
        ("z", "x", "y", "core"),
    )
    tokens = ("y", "core", "z", "x")
    placed = (
        P(tokens, None),
        P(tokens, None),
        P(tokens, None),
        P(tokens, None),
        P(tokens),
        P(tokens),
        P(),
        P(),
        P(),
        P(("z", "x"), None),
        P(("z", "x", "y", "core"), None),
        P(("z", "x", "y", "core"), None),
    )
    return jax.shard_map(
        step,
        mesh=fine,
        in_specs=placed,
        out_specs=(
            P(tokens, None),
            P(("z", "x"), None),
            P(("z", "x", "y", "core"), None),
            P(("z", "x", "y", "core"), None),
        ),
        check_vma=False,
    )
```

```python
import functools
import math

import jax
import jax.numpy as jnp
from jax import lax
from jax.experimental import pallas as pl
from jax.experimental.pallas import tpu as pltpu
from jax.sharding import Mesh
from jax.sharding import PartitionSpec as P


HEAD = 128
ROLLS = 2
PAIR = 2


clip_low = 0.8
clip_high = 1.2
decay_first = 0.9
decay_second = 0.95
step_rate = 0.001
weight_decay = 0.1
adam_eps = 1e-08
bias_first = 1.0 - 0.9**10
bias_second = 1.0 - 0.95**10

ROOM = pltpu.CompilerParams(vmem_limit_bytes=16 * 2**20)


def coefficient_kernel(full_len, place, rewards, group_ids, lengths, new_lp, old_lp, out):
    count_all = rewards.shape[0]
    shape = out.shape
    half = shape[1] // ROLLS
    lane = lax.broadcasted_iota(jnp.int32, shape, 1)
    adv_tok = jnp.zeros(shape, jnp.float32)
    len_tok = jnp.zeros(shape, jnp.int32)
    pos_tok = lane + (place[0] * PAIR + place[1]) * half
    for roll in range(ROLLS):
        mine = (place[2] * 2 + place[3]) * ROLLS + roll
        same = [group_ids[n] == group_ids[mine] for n in range(count_all)]
        values = [jnp.full(shape, rewards[n], jnp.float32) for n in range(count_all)]
        count = sum(jnp.full(shape, jnp.where(flag, 1.0, 0.0), jnp.float32) for flag in same)
        mean = sum(jnp.where(flag, value, 0.0) for flag, value in zip(same, values)) / count
        variance = (
            sum(
                jnp.where(flag, (value - mean) * (value - mean), 0.0)
                for flag, value in zip(same, values)
            )
            / count
        )
        spread = jnp.full(shape, rewards[mine], jnp.float32) - mean
        advantage = spread / jnp.maximum(jnp.sqrt(variance), 1.0)
        here = (lane >= roll * half) & (lane < (roll + 1) * half)
        adv_tok = jnp.where(here, advantage, adv_tok)
        len_tok = jnp.where(here, lengths[mine], len_tok)
        pos_tok = jnp.where(here, pos_tok - roll * half, pos_tok)
    ratio_now = jnp.exp(new_lp[...] - old_lp[...])
    clipped = jnp.clip(ratio_now, clip_low, clip_high)
    active = (ratio_now * adv_tok <= clipped * adv_tok) & (pos_tok < len_tok)
    len_weight = full_len / len_tok.astype(jnp.float32)
    out[...] = jnp.where(active, -adv_tok * ratio_now * len_weight, 0.0)


def coefficients(place, rewards, group_ids, lengths, new_logp, old_logp, full_len):
    shape = (1, new_logp.shape[0])
    scalars = pl.BlockSpec(memory_space=pltpu.SMEM)
    whole = pl.BlockSpec(memory_space=pltpu.VMEM)
    return pl.pallas_call(
        functools.partial(coefficient_kernel, full_len),
        in_specs=[scalars] * 4 + [whole] * 2,
        out_specs=whole,
        out_shape=jax.ShapeDtypeStruct(shape, jnp.float32),
        compiler_params=ROOM,
    )(place, rewards, group_ids, lengths, new_logp.reshape(shape), old_logp.reshape(shape))


def attention_kernel(slots, half, place, q_own, q_far, g_own, g_far, c_own, c_far, *refs):
    key_refs, part_refs, probs = refs[:slots], refs[slots : 2 * slots], refs[2 * slots]
    z_index, x_index = place[0], place[1]
    per_group = q_own.shape[1] // HEAD
    block = PAIR * half
    scale = math.log2(math.e) / math.sqrt(HEAD)

    def spot(dim):
        at = lax.broadcasted_iota(jnp.int32, (block, block), dim)
        return jnp.where(at < half, at + x_index * half, at - half + (1 - x_index) * half)

    causal = spot(0) <= spot(1)
    for roll in range(ROLLS):
        rows = slice(roll * half, (roll + 1) * half)
        far_rows = slice((ROLLS + roll) * half, (ROLLS + roll + 1) * half)
        keys = jnp.concatenate(
            [key_refs[n][part, :] for n in range(slots) for part in (rows, far_rows)], axis=0
        )
        grads = []
        coeff = jnp.concatenate([c_own[:, rows], c_far[:, rows]], axis=1)
        for head in range(per_group):
            cols = slice(head * HEAD, (head + 1) * HEAD)
            query = jnp.concatenate([q_own[rows, cols], q_far[rows, cols]], axis=0)
            grads += [g_own[rows, cols], g_far[rows, cols]]
            scores = (
                lax.dot_general(
                    keys, query, (((1,), (1,)), ((), ())), preferred_element_type=jnp.float32
                )
                * scale
            )
            pieces = [jnp.where(causal, scores[:block], -1e30)]
            for n in range(1, slots):
                pieces.append(
                    jnp.where(z_index >= n, scores[n * block : (n + 1) * block], -1e30)
                )
            top = functools.reduce(
                jnp.maximum, [jnp.max(piece, axis=0, keepdims=True) for piece in pieces]
            )
            expo = [jnp.exp2(piece - top) for piece in pieces]
            total = sum(jnp.sum(piece, axis=0, keepdims=True) for piece in expo)
            weight = coeff / total
            for n in range(slots):
                probs[n * block : (n + 1) * block, head * block : (head + 1) * block] = (
                    expo[n] * weight
                ).astype(jnp.bfloat16)
        summed = jnp.dot(
            probs[...], jnp.concatenate(grads, axis=0), preferred_element_type=jnp.float32
        ).astype(jnp.bfloat16)
        for n in range(slots):
            part_refs[n][rows, :] = summed[n * block : n * block + half]
            part_refs[n][far_rows, :] = summed[n * block + half : (n + 1) * block]


def attention_parts(place, queries, q_far, logp_grad, g_far, c_own, c_far, key_blocks):
    slots = len(key_blocks)
    tok_rows, q_cols = q_far.shape
    kv_heads = key_blocks[0].shape[1] // HEAD
    per_head = q_cols // kv_heads
    half = tok_rows // ROLLS
    own_spec = pl.BlockSpec((tok_rows, per_head), lambda h, place: (0, place[1] * kv_heads + h))
    far_spec = pl.BlockSpec((tok_rows, per_head), lambda h, place: (0, h))
    coeff_spec = pl.BlockSpec(c_own.shape, lambda h, place: (0, 0))
    k_spec = pl.BlockSpec((PAIR * tok_rows, HEAD), lambda h, place: (0, h))
    shape = jax.ShapeDtypeStruct(key_blocks[0].shape, jnp.bfloat16)
    work = 4 * kv_heads * per_head * ROLLS * (PAIR * half) ** 2 * slots
    return pl.pallas_call(
        functools.partial(attention_kernel, slots, half),
        grid_spec=pltpu.PrefetchScalarGridSpec(
            num_scalar_prefetch=1,
            grid=(kv_heads,),
            in_specs=[own_spec, far_spec] * 2 + [coeff_spec] * 2 + [k_spec] * slots,
            out_specs=[k_spec] * slots,
            scratch_shapes=[
                pltpu.VMEM(
                    (slots * PAIR * half, per_head // HEAD * PAIR * half), jnp.bfloat16
                )
            ],
        ),
        out_shape=[shape] * slots,
        compiler_params=ROOM,
        cost_estimate=pl.CostEstimate(
            flops=work, bytes_accessed=8 * tok_rows * q_cols, transcendentals=work // 256
        ),
    )(place, queries, q_far, logp_grad, g_far, c_own, c_far, *key_blocks)


def pack_kernel(tok_rows, keys, queries, grads, key_room, k_far, q_far, g_far, sems):
    x_index = lax.axis_index("x")

    def half(array, index):
        cols = array.shape[1] // PAIR
        return array.at[:, pl.ds(pl.multiple_of(index * cols, HEAD), cols)]

    copies = [
        pltpu.make_async_copy(source, target, sems.at[n])
        for n, (source, target) in enumerate(
            [
                (half(keys, 1 - x_index), k_far),
                (half(keys, x_index), key_room.at[pl.ds(0, tok_rows), :]),
                (half(queries, 1 - x_index), q_far),
                (half(grads, 1 - x_index), g_far),
            ]
        )
    ]
    for copy in copies:
        copy.start()
    for copy in copies:
        copy.wait()


def packed(key_vectors, queries, logp_grad):
    tok_rows = queries.shape[0]

    def half(array, rows):
        return jax.ShapeDtypeStruct((rows, array.shape[1] // PAIR), jnp.bfloat16)

    return pl.pallas_call(
        functools.partial(pack_kernel, tok_rows),
        in_specs=[pl.BlockSpec(memory_space=pl.ANY)] * 3,
        out_specs=[pl.BlockSpec(memory_space=pltpu.VMEM)] * 4,
        out_shape=[
            half(key_vectors, PAIR * tok_rows),
            half(key_vectors, tok_rows),
            half(queries, tok_rows),
            half(logp_grad, tok_rows),
        ],
        scratch_shapes=[pltpu.SemaphoreType.DMA((4,))],
        cost_estimate=pl.CostEstimate(
            flops=0, bytes_accessed=4 * queries.size, transcendentals=0
        ),
    )(key_vectors, queries, logp_grad)


def owner_kernel(pieces, z_size, place, near, far, *refs):
    values, outs = refs[: 2 * pieces], refs[2 * pieces : 2 * pieces + z_size]
    token_rows = refs[2 * pieces + z_size]
    buffers, totals, sems = refs[-3:]
    copies = [
        pltpu.make_async_copy(source, buffers.at[n], sems.at[n])
        for n, source in enumerate((near, far))
    ]
    for copy in copies:
        copy.start()
    sides = near.shape[0] // PAIR
    rows, tokens = near.shape[2:]
    half = values[0].shape[1]
    for n, copy in enumerate(copies):
        copy.wait()
        for m in range(PAIR):
            columns = jnp.concatenate(
                [
                    buffers[n, (x + m) % PAIR * sides + y].reshape(z_size * rows, tokens)
                    for y in range(sides)
                    for x in range(PAIR)
                ],
                axis=1,
            )
            blocks = values[m * pieces + n * sides : m * pieces + (n + 1) * sides]
            product = jnp.dot(
                columns,
                jnp.concatenate([ref[...] for ref in blocks], axis=0),
                preferred_element_type=jnp.float32,
            )
            part = slice(m * half, (m + 1) * half)
            totals[:, part] = product if n == 0 else totals[:, part] + product
    flag = place[1] == 0
    for x in range(PAIR):
        for y in range(sides):
            low = values[y][x * tokens : (x + 1) * tokens, :]
            high = values[pieces + y][(1 - x) * tokens : (2 - x) * tokens, :]
            at = (x * sides + y) * tokens
            token_rows[at : at + tokens, :half] = jnp.where(flag, low, high)
            token_rows[at : at + tokens, half:] = jnp.where(flag, high, low)
    for k, out in enumerate(outs):
        at = place[0] + k
        start = pl.multiple_of(jnp.where(at >= z_size, at - z_size, at) * rows, rows)
        out[...] = totals[pl.ds(start, rows), :].astype(jnp.bfloat16)


def plain_owner_products(place, near, far, first, second):
    z_size, rows, tokens = near.shape[1:]
    sides = near.shape[0] // PAIR
    halves = []
    for m, blocks in enumerate((first, second)):
        total = 0.0
        for n, array in enumerate((near, far)):
            order = [(x + m) % PAIR * sides + y for y in range(sides) for x in range(PAIR)]
            columns = jnp.stack([array[at] for at in order], axis=2)
            total = total + jnp.dot(
                columns.reshape(z_size * rows, -1),
                jnp.concatenate(blocks[n * sides : (n + 1) * sides], axis=0),
                preferred_element_type=jnp.float32,
            )
        halves.append(total.astype(jnp.bfloat16))
    every = jnp.concatenate(halves, axis=1).reshape(z_size, rows, -1)
    groups = []
    for x in range(PAIR):
        for y in range(sides):
            low = first[y][x * tokens : (x + 1) * tokens]
            high = second[y][(1 - x) * tokens : (2 - x) * tokens]
            groups.append(
                jnp.where(
                    place[1] == 0,
                    jnp.concatenate([low, high], axis=1),
                    jnp.concatenate([high, low], axis=1),
                )
            )
    return [cut(every, turned(place[0], k, z_size), 0) for k in range(z_size)] + [
        jnp.concatenate(groups, axis=0)
    ]


def owner_products(place, near, far, first, second):
    z_size, rows, tokens = near.shape[1:]
    if rows % 16:
        return plain_owner_products(place, near, far, first, second)
    pieces = len(first)
    width = 2 * first[0].shape[1]
    whole = pl.BlockSpec(memory_space=pltpu.VMEM)
    shape = jax.ShapeDtypeStruct((rows, width), jnp.bfloat16)
    return pl.pallas_call(
        functools.partial(owner_kernel, pieces, z_size),
        in_specs=[pl.BlockSpec(memory_space=pltpu.SMEM)]
        + [pl.BlockSpec(memory_space=pl.ANY)] * 2
        + [whole] * (2 * pieces),
        out_specs=[whole] * (z_size + 1),
        out_shape=[shape] * z_size
        + [jax.ShapeDtypeStruct((near.shape[0] * tokens, width), jnp.bfloat16)],
        scratch_shapes=[
            pltpu.VMEM((2, *near.shape), jnp.bfloat16),
            pltpu.VMEM((z_size * rows, width), jnp.float32),
            pltpu.SemaphoreType.DMA((2,)),
        ],
        compiler_params=ROOM,
        cost_estimate=pl.CostEstimate(
            flops=4 * near.size * width, bytes_accessed=8 * near.size, transcendentals=0
        ),
    )(place, near, far, *first, *second)


def row_kernel(z_size, groups, place, token_rows, *refs):
    proj, outs = refs[:4], refs[4 : 4 + groups]
    rows_all, sems = refs[-2:]
    rows, tok_rows = proj[0].shape[1], outs[0].shape[0]
    copies = []
    for k, bits in enumerate(flips(z_size)):
        for c in range(2):
            at_core = place[3] if c == 0 else 1 - place[3]
            start = ((place[0] ^ bits) * 2 + at_core) * rows
            group, at = divmod(k, z_size // 2)
            copies.append(
                pltpu.make_async_copy(
                    proj[2 * c + group].at[at],
                    rows_all.at[pl.ds(pl.multiple_of(start, rows), rows), :],
                    sems.at[2 * k + c],
                )
            )
    for copy in copies:
        copy.start()
    for copy in copies:
        copy.wait()
    product = lax.dot_general(
        token_rows[...],
        rows_all[...],
        (((1,), (1,)), ((), ())),
        preferred_element_type=jnp.float32,
    ).astype(jnp.bfloat16)
    for n, out in enumerate(outs):
        out[...] = product[n * tok_rows : (n + 1) * tok_rows]


def plane_kernel(place, columns, *outs):
    y_size = columns.shape[2]
    for x in range(PAIR):
        for y in range(y_size):
            at_x, at_y = place[1] + x, place[2] + y
            at_x = jnp.where(at_x >= PAIR, at_x - PAIR, at_x)
            at_y = jnp.where(at_y >= y_size, at_y - y_size, at_y)
            out = outs[x * y_size + y]
            for z in range(columns.shape[0]):
                out[z] = columns[z, at_x, at_y]


def core_kernel(place, *refs):
    pieces, (near, far) = refs[:-2], refs[-2:]
    for n, piece in enumerate(pieces):
        for z in range(piece.shape[0]):
            near[n, z] = piece[z, place[3]]
            far[n, z] = piece[z, 1 - place[3]]


def sliced(kernel, place, arrays, shapes):
    whole = pl.BlockSpec(memory_space=pltpu.VMEM)
    return pl.pallas_call(
        kernel,
        in_specs=[pl.BlockSpec(memory_space=pltpu.SMEM)] + [whole] * len(arrays),
        out_specs=[whole] * len(shapes),
        out_shape=[jax.ShapeDtypeStruct(shape, jnp.bfloat16) for shape in shapes],
        compiler_params=ROOM,
        cost_estimate=pl.CostEstimate(
            flops=0,
            bytes_accessed=4 * sum(math.prod(shape) for shape in shapes),
            transcendentals=0,
        ),
    )(place, *arrays)


def by_place(blocks, index):
    size = len(blocks)
    back = jnp.stack([blocks[-k % size] for k in range(size)])
    start = jnp.where(index == 0, 0, size - index)
    return lax.dynamic_slice_in_dim(jnp.concatenate([back, back], axis=0), start, size, 0)


def plain_row_products(place, token_rows, groups, proj):
    width = proj[0].shape[2]
    z_size = 2 * proj[0].shape[0]
    cores = by_place(
        [jnp.concatenate(proj[2 * c : 2 * c + 2], axis=0) for c in range(2)], place[3]
    )
    order = {bits: k for k, bits in enumerate(flips(z_size))}
    along = jnp.stack([cores[:, order[k]] for k in range(z_size)])
    along = jnp.take(along, jnp.arange(z_size, dtype=jnp.int32) ^ place[0], axis=0)
    every = along.reshape(-1, width)
    product = jnp.dot(token_rows, every.T, preferred_element_type=jnp.float32)
    return jnp.split(product.astype(jnp.bfloat16), groups)


def row_products(place, token_rows, groups, proj):
    _, rows, width = proj[0].shape
    z_size = 2 * proj[0].shape[0]
    tok_rows = token_rows.shape[0] // groups
    cols = 2 * z_size * rows
    if rows % 16 or cols % 128:
        return plain_row_products(place, token_rows, groups, proj)
    whole = pl.BlockSpec(memory_space=pltpu.VMEM)
    shape = jax.ShapeDtypeStruct((tok_rows, cols), jnp.bfloat16)
    return pl.pallas_call(
        functools.partial(row_kernel, z_size, groups),
        in_specs=[pl.BlockSpec(memory_space=pltpu.SMEM), whole]
        + [pl.BlockSpec(memory_space=pl.ANY)] * len(proj),
        out_specs=[whole] * groups,
        out_shape=[shape] * groups,
        scratch_shapes=[
            pltpu.VMEM((cols, width), jnp.bfloat16),
            pltpu.SemaphoreType.DMA((2 * z_size,)),
        ],
        compiler_params=ROOM,
        cost_estimate=pl.CostEstimate(
            flops=2 * groups * tok_rows * width * cols,
            bytes_accessed=2 * cols * (width + groups * tok_rows),
            transcendentals=0,
        ),
    )(place, token_rows, *proj)


def final_kernel(z_size, place, *refs):
    pieces, out = refs[:-1], refs[-1]
    cols = pieces[0].shape[1] // z_size
    flags = place[1] == 0, place[2] == 0
    for z in range(z_size):
        part = slice(z * cols, (z + 1) * cols)
        near = [jnp.where(flags[1], pieces[y][:, part], pieces[1 - y][:, part]) for y in (0, 1)]
        far = [
            jnp.where(flags[1], pieces[2 + y][:, part], pieces[3 - y][:, part]) for y in (0, 1)
        ]
        near, far = jnp.concatenate(near, axis=1), jnp.concatenate(far, axis=1)
        wide = 2 * cols
        out[:, 2 * z * wide : (2 * z + 1) * wide] = jnp.where(flags[0], near, far)
        out[:, (2 * z + 1) * wide : (2 * z + 2) * wide] = jnp.where(flags[0], far, near)


def assembled(place, pieces, z_size):
    tokens = pieces[0].shape[0]
    y_size = len(pieces) // PAIR
    cols = pieces[0].shape[1] // z_size
    if y_size != 2 or 2 * cols % 128:
        split = [piece.reshape(tokens, z_size, cols) for piece in pieces]
        both = []
        for x in range(PAIR):
            found = jnp.stack(split[x * y_size : (x + 1) * y_size])
            start = jnp.where(place[2] == 0, 0, y_size - place[2])
            both.append(
                lax.dynamic_slice_in_dim(
                    jnp.concatenate([found, found], axis=0), start, y_size, 0
                )
            )
        both = jnp.stack(both)
        both = jnp.where(place[1] == 0, both, both[::-1])
        return both.transpose(2, 3, 0, 1, 4).reshape(tokens, -1)
    steps = 2 if tokens % 64 == 0 else 1

    def rows(array_cols):
        return pl.BlockSpec((tokens // steps, array_cols), lambda i, place: (i, 0))

    return pl.pallas_call(
        functools.partial(final_kernel, z_size),
        grid_spec=pltpu.PrefetchScalarGridSpec(
            num_scalar_prefetch=1,
            grid=(steps,),
            in_specs=[rows(z_size * cols)] * len(pieces),
            out_specs=rows(len(pieces) * z_size * cols),
        ),
        out_shape=jax.ShapeDtypeStruct((tokens, len(pieces) * z_size * cols), jnp.bfloat16),
        compiler_params=ROOM,
        cost_estimate=pl.CostEstimate(
            flops=0, bytes_accessed=4 * tokens * len(pieces) * z_size * cols, transcendentals=0
        ),
    )(place, *pieces)


def adam_rows(old_rows, grad_rows, first_moment, second_moment):
    first = decay_first * first_moment.astype(jnp.float32) + (1.0 - decay_first) * grad_rows
    second = (
        decay_second * second_moment.astype(jnp.float32)
        + (1.0 - decay_second) * grad_rows * grad_rows
    )
    weight_now = old_rows.astype(jnp.float32)
    update = (
        first / bias_first / (jnp.sqrt(second / bias_second) + adam_eps) + weight_decay * weight_now
    )
    return (
        (weight_now - step_rate * update).astype(jnp.bfloat16),
        first.astype(jnp.bfloat16),
        second.astype(jnp.bfloat16),
    )


def adam_kernel(place, count, *refs):
    pieces, (old_rows, first_moment, second_moment), outs = refs[:count], refs[count:-3], refs[-3:]
    grad = pieces[0][...].astype(jnp.float32)
    for piece in pieces[1:]:
        grad = grad + piece[...].astype(jnp.float32)
    mid = grad.shape[1] // 2
    swap = jnp.concatenate([grad[:, mid:], grad[:, :mid]], axis=1)
    grad = jnp.where(place[1] == 0, grad, swap)
    for out, value in zip(
        outs, adam_rows(old_rows[...], grad, first_moment[...], second_moment[...])
    ):
        out[...] = value


def adam_step(place, pieces, old_rows, first_moment, second_moment):
    arrays = [*pieces, old_rows, first_moment, second_moment]
    whole = pl.BlockSpec(memory_space=pltpu.VMEM)
    return pl.pallas_call(
        lambda place, *refs: adam_kernel(place, len(pieces), *refs),
        in_specs=[pl.BlockSpec(memory_space=pltpu.SMEM)] + [whole] * len(arrays),
        out_specs=[whole] * 3,
        out_shape=[jax.ShapeDtypeStruct(old_rows.shape, jnp.bfloat16)] * 3,
        compiler_params=ROOM,
        cost_estimate=pl.CostEstimate(
            flops=40 * old_rows.size,
            bytes_accessed=2 * (len(arrays) + 3) * old_rows.size,
            transcendentals=old_rows.size,
        ),
    )(place, *arrays)


def shift(value, axis, step, wrap=True):
    size = lax.axis_size(axis)
    pairs = [(i, (i + step) % size) for i in range(size) if wrap or 0 <= i + step < size]
    return lax.ppermute(value, axis, pairs)


def turned(index, step, size):
    moved = index + step
    return jnp.where(moved >= size, moved - size, moved)


def z_bits(z_size):
    assert z_size & (z_size - 1) == 0
    return [1 << n for n in range(z_size.bit_length() - 2, -1, -1)]


def flips(z_size):
    bits = z_bits(z_size)
    return [
        functools.reduce(int.__xor__, [bit for n, bit in enumerate(bits) if k >> n & 1], 0)
        for k in range(z_size)
    ]


def cut(value, index, dim):
    return lax.dynamic_index_in_dim(value, index, dim, keepdims=False)


def step(
    attn_inputs,
    queries,
    key_vectors,
    logp_grad,
    new_logp,
    old_logp,
    rewards,
    group_ids,
    lengths,
    value_proj,
    first_moment,
    second_moment,
):
    z_size, y_size, core_size = lax.axis_size("z"), lax.axis_size("y"), lax.axis_size("core")
    z_index, x_index = lax.axis_index("z"), lax.axis_index("x")
    side_index = lax.axis_index("y") * core_size + lax.axis_index("core")
    tok_rows, _ = attn_inputs.shape
    half = tok_rows // ROLLS
    full_len = half * z_size * PAIR
    shard_rows = first_moment.shape[0]
    y_index, core_index = lax.axis_index("y"), lax.axis_index("core")
    place = jnp.stack([z_index, x_index, y_index, core_index]).astype(jnp.int32)

    key_room, key_out, q_out, g_out = packed(key_vectors, queries, logp_grad)
    key_far = shift(key_out, "x", 1)
    q_far = shift(q_out, "x", 1)
    g_far = shift(g_out, "x", 1)
    key_block = lax.dynamic_update_slice(key_room, key_far, (tok_rows, 0))
    key_blocks = [key_block] + [shift(key_block, "z", k, False) for k in range(1, z_size)]
    columns = attn_inputs.T.reshape(z_size, PAIR, y_size, core_size, shard_rows, tok_rows)
    found = []
    block = (z_size, core_size, shard_rows, tok_rows)
    cuts = sliced(plane_kernel, place, [columns], [block] * (PAIR * y_size))
    for x in range(PAIR):
        for k in range(y_size):
            piece = cuts[x * y_size + k]
            if x or k:
                pairs = [
                    (a * y_size + b, (a + x) % PAIR * y_size + (b + k) % y_size)
                    for a in range(PAIR)
                    for b in range(y_size)
                ]
                piece = lax.ppermute(piece, ("x", "y"), pairs)
            found.append(piece)
    every = (PAIR * y_size, z_size, shard_rows, tok_rows)
    near_cols, far_cols = sliced(core_kernel, place, found, [every] * 2)
    far_cols = shift(far_cols, "core", 1)

    coeff = coefficients(
        place, rewards, group_ids, lengths, new_logp, old_logp, full_len
    )
    coeff_far = shift(coeff, "x", 1)

    own_proj = lax.dynamic_slice_in_dim(value_proj, side_index * shard_rows, shard_rows, 0)
    own_proj = lax.optimization_barrier(own_proj)
    bits = z_bits(z_size)
    known = own_proj[None]
    for n, bit in enumerate(bits):
        pairs = [(i, i ^ bit) for i in range(z_size)]
        arrived = lax.ppermute(known, "z", pairs)
        if n < len(bits) - 1:
            known = jnp.concatenate([known, arrived], axis=0)
    proj = [known, arrived, shift(known, "core", 1), shift(arrived, "core", 1)]

    parts = attention_parts(place, queries, q_far, logp_grad, g_far, coeff, coeff_far, key_blocks)
    total = parts[0].astype(jnp.float32)
    for k in range(1, z_size):
        arrived = shift(parts[k], "z", -k, False)
        total = total + arrived.astype(jnp.float32)

    def over_sides(value):
        found = [value] + [shift(value, "y", k) for k in range(1, y_size)]
        return found + [shift(block, "core", 1) for block in found]

    first_cols = total.astype(jnp.bfloat16)
    second_cols = shift(first_cols, "x", 1)
    first_all = over_sides(first_cols)
    second_all = over_sides(second_cols)

    pieces = owner_products(place, near_cols, far_cols, first_all, second_all)
    arrived_sums = [shift(pieces[k], "z", k) for k in range(1, z_size)]
    products = row_products(place, pieces[z_size], PAIR * y_size, proj)
    back = list(products)
    for k in range(1, y_size):
        back[k] = shift(products[k], "y", -k)
    back[y_size] = shift(products[y_size], "x", 1)
    for k in range(1, y_size):
        pairs = [
            (x * y_size + y, (1 - x) * y_size + (y - k) % y_size)
            for x in range(PAIR)
            for y in range(y_size)
        ]
        back[y_size + k] = lax.ppermute(products[y_size + k], ("x", "y"), pairs)
    input_grad = assembled(place, back, z_size)

    new_rows, new_first, new_second = adam_step(
        place, [pieces[0], *arrived_sums], own_proj, first_moment, second_moment
    )
    sides = [new_rows] + [shift(new_rows, "y", k) for k in range(1, y_size)]
    others = [shift(block, "core", 1) for block in sides]
    if y_size == 2:
        columns = [
            [jnp.where(y_index == 0, blocks[y], blocks[1 - y]) for y in range(2)]
            for blocks in (sides, others)
        ]
    else:
        columns = [list(by_place(blocks, y_index)) for blocks in (sides, others)]
    new_proj = jnp.concatenate(
        [
            jnp.where(core_index == c, columns[0][y], columns[1][y])
            for y in range(y_size)
            for c in range(core_size)
        ],
        axis=0,
    )
    return (input_grad, new_proj, new_first, new_second)


def solution(mesh):
    fsdp_size, side_size = mesh.shape["fsdp"], mesh.shape["side"]
    fine = Mesh(
        mesh.devices.reshape(fsdp_size // PAIR, PAIR, side_size // 2, 2),
        ("z", "x", "y", "core"),
    )
    tokens = ("y", "core", "z", "x")
    placed = (
        P(tokens, None),
        P(tokens, None),
        P(tokens, None),
        P(tokens, None),
        P(tokens),
        P(tokens),
        P(),
        P(),
        P(),
        P(("z", "x"), None),
        P(("z", "x", "y", "core"), None),
        P(("z", "x", "y", "core"), None),
    )
    return jax.shard_map(
        step,
        mesh=fine,
        in_specs=placed,
        out_specs=(
            P(tokens, None),
            P(("z", "x"), None),
            P(("z", "x", "y", "core"), None),
            P(("z", "x", "y", "core"), None),
        ),
        check_vma=False,
    )
```

```python
import functools
import math

import jax
import jax.numpy as jnp
from jax import lax
from jax.experimental import pallas as pl
from jax.experimental.pallas import tpu as pltpu
from jax.sharding import Mesh
from jax.sharding import PartitionSpec as P


HEAD = 128
ROLLS = 2
PAIR = 2


clip_low = 0.8
clip_high = 1.2
decay_first = 0.9
decay_second = 0.95
step_rate = 0.001
weight_decay = 0.1
adam_eps = 1e-08
bias_first = 1.0 - 0.9**10
bias_second = 1.0 - 0.95**10

ROOM = pltpu.CompilerParams(vmem_limit_bytes=16 * 2**20)


def coefficient_kernel(full_len, place, rewards, group_ids, lengths, new_lp, old_lp, out):
    count_all = rewards.shape[0]
    shape = out.shape
    half = shape[1] // ROLLS
    lane = lax.broadcasted_iota(jnp.int32, shape, 1)
    adv_tok = jnp.zeros(shape, jnp.float32)
    len_tok = jnp.zeros(shape, jnp.int32)
    pos_tok = lane + (place[0] * PAIR + place[1]) * half
    for roll in range(ROLLS):
        mine = (place[2] * 2 + place[3]) * ROLLS + roll
        same = [group_ids[n] == group_ids[mine] for n in range(count_all)]
        values = [jnp.full(shape, rewards[n], jnp.float32) for n in range(count_all)]
        count = sum(jnp.full(shape, jnp.where(flag, 1.0, 0.0), jnp.float32) for flag in same)
        mean = sum(jnp.where(flag, value, 0.0) for flag, value in zip(same, values)) / count
        variance = (
            sum(
                jnp.where(flag, (value - mean) * (value - mean), 0.0)
                for flag, value in zip(same, values)
            )
            / count
        )
        spread = jnp.full(shape, rewards[mine], jnp.float32) - mean
        advantage = spread / jnp.maximum(jnp.sqrt(variance), 1.0)
        here = (lane >= roll * half) & (lane < (roll + 1) * half)
        adv_tok = jnp.where(here, advantage, adv_tok)
        len_tok = jnp.where(here, lengths[mine], len_tok)
        pos_tok = jnp.where(here, pos_tok - roll * half, pos_tok)
    ratio_now = jnp.exp(new_lp[...] - old_lp[...])
    clipped = jnp.clip(ratio_now, clip_low, clip_high)
    active = (ratio_now * adv_tok <= clipped * adv_tok) & (pos_tok < len_tok)
    len_weight = full_len / len_tok.astype(jnp.float32)
    out[...] = jnp.where(active, -adv_tok * ratio_now * len_weight, 0.0)


def coefficients(place, rewards, group_ids, lengths, new_logp, old_logp, full_len):
    shape = (1, new_logp.shape[0])
    scalars = pl.BlockSpec(memory_space=pltpu.SMEM)
    whole = pl.BlockSpec(memory_space=pltpu.VMEM)
    return pl.pallas_call(
        functools.partial(coefficient_kernel, full_len),
        in_specs=[scalars] * 4 + [whole] * 2,
        out_specs=whole,
        out_shape=jax.ShapeDtypeStruct(shape, jnp.float32),
        compiler_params=ROOM,
    )(place, rewards, group_ids, lengths, new_logp.reshape(shape), old_logp.reshape(shape))


def attention_kernel(slots, half, place, q_own, q_far, g_own, g_far, c_own, c_far, *refs):
    key_refs, part_refs, probs = refs[:slots], refs[slots : 2 * slots], refs[2 * slots]
    z_index, x_index = place[0], place[1]
    per_group = q_own.shape[1] // HEAD
    block = PAIR * half
    scale = math.log2(math.e) / math.sqrt(HEAD)

    def spot(dim):
        at = lax.broadcasted_iota(jnp.int32, (block, block), dim)
        return jnp.where(at < half, at + x_index * half, at - half + (1 - x_index) * half)

    causal = spot(0) <= spot(1)
    for roll in range(ROLLS):
        rows = slice(roll * half, (roll + 1) * half)
        far_rows = slice((ROLLS + roll) * half, (ROLLS + roll + 1) * half)
        keys = jnp.concatenate(
            [key_refs[n][part, :] for n in range(slots) for part in (rows, far_rows)], axis=0
        )
        grads = []
        coeff = jnp.concatenate([c_own[:, rows], c_far[:, rows]], axis=1)
        for head in range(per_group):
            cols = slice(head * HEAD, (head + 1) * HEAD)
            query = jnp.concatenate([q_own[rows, cols], q_far[rows, cols]], axis=0)
            grads += [g_own[rows, cols], g_far[rows, cols]]
            scores = (
                lax.dot_general(
                    keys, query, (((1,), (1,)), ((), ())), preferred_element_type=jnp.float32
                )
                * scale
            )
            pieces = [jnp.where(causal, scores[:block], -1e30)]
            for n in range(1, slots):
                pieces.append(
                    jnp.where(z_index >= n, scores[n * block : (n + 1) * block], -1e30)
                )
            top = functools.reduce(
                jnp.maximum, [jnp.max(piece, axis=0, keepdims=True) for piece in pieces]
            )
            expo = [jnp.exp2(piece - top) for piece in pieces]
            total = sum(jnp.sum(piece, axis=0, keepdims=True) for piece in expo)
            weight = coeff / total
            for n in range(slots):
                probs[n * block : (n + 1) * block, head * block : (head + 1) * block] = (
                    expo[n] * weight
                ).astype(jnp.bfloat16)
        summed = jnp.dot(
            probs[...], jnp.concatenate(grads, axis=0), preferred_element_type=jnp.float32
        ).astype(jnp.bfloat16)
        for n in range(slots):
            part_refs[n][rows, :] = summed[n * block : n * block + half]
            part_refs[n][far_rows, :] = summed[n * block + half : (n + 1) * block]


def attention_parts(place, queries, q_far, logp_grad, g_far, c_own, c_far, key_blocks):
    slots = len(key_blocks)
    tok_rows, q_cols = q_far.shape
    kv_heads = key_blocks[0].shape[1] // HEAD
    per_head = q_cols // kv_heads
    half = tok_rows // ROLLS
    own_spec = pl.BlockSpec((tok_rows, per_head), lambda h, place: (0, place[1] * kv_heads + h))
    far_spec = pl.BlockSpec((tok_rows, per_head), lambda h, place: (0, h))
    coeff_spec = pl.BlockSpec(c_own.shape, lambda h, place: (0, 0))
    k_spec = pl.BlockSpec((PAIR * tok_rows, HEAD), lambda h, place: (0, h))
    shape = jax.ShapeDtypeStruct(key_blocks[0].shape, jnp.bfloat16)
    work = 4 * kv_heads * per_head * ROLLS * (PAIR * half) ** 2 * slots
    return pl.pallas_call(
        functools.partial(attention_kernel, slots, half),
        grid_spec=pltpu.PrefetchScalarGridSpec(
            num_scalar_prefetch=1,
            grid=(kv_heads,),
            in_specs=[own_spec, far_spec] * 2 + [coeff_spec] * 2 + [k_spec] * slots,
            out_specs=[k_spec] * slots,
            scratch_shapes=[
                pltpu.VMEM(
                    (slots * PAIR * half, per_head // HEAD * PAIR * half), jnp.bfloat16
                )
            ],
        ),
        out_shape=[shape] * slots,
        compiler_params=ROOM,
        cost_estimate=pl.CostEstimate(
            flops=work, bytes_accessed=8 * tok_rows * q_cols, transcendentals=work // 256
        ),
    )(place, queries, q_far, logp_grad, g_far, c_own, c_far, *key_blocks)


def pack_kernel(tok_rows, keys, queries, grads, key_room, k_far, q_far, g_far, sems):
    x_index = lax.axis_index("x")

    def half(array, index):
        cols = array.shape[1] // PAIR
        return array.at[:, pl.ds(pl.multiple_of(index * cols, HEAD), cols)]

    copies = [
        pltpu.make_async_copy(source, target, sems.at[n])
        for n, (source, target) in enumerate(
            [
                (half(keys, 1 - x_index), k_far),
                (half(keys, x_index), key_room.at[pl.ds(0, tok_rows), :]),
                (half(queries, 1 - x_index), q_far),
                (half(grads, 1 - x_index), g_far),
            ]
        )
    ]
    for copy in copies:
        copy.start()
    for copy in copies:
        copy.wait()


def packed(key_vectors, queries, logp_grad):
    tok_rows = queries.shape[0]

    def half(array, rows):
        return jax.ShapeDtypeStruct((rows, array.shape[1] // PAIR), jnp.bfloat16)

    return pl.pallas_call(
        functools.partial(pack_kernel, tok_rows),
        in_specs=[pl.BlockSpec(memory_space=pl.ANY)] * 3,
        out_specs=[pl.BlockSpec(memory_space=pltpu.VMEM)] * 4,
        out_shape=[
            half(key_vectors, PAIR * tok_rows),
            half(key_vectors, tok_rows),
            half(queries, tok_rows),
            half(logp_grad, tok_rows),
        ],
        scratch_shapes=[pltpu.SemaphoreType.DMA((4,))],
        cost_estimate=pl.CostEstimate(
            flops=0, bytes_accessed=4 * queries.size, transcendentals=0
        ),
    )(key_vectors, queries, logp_grad)


def owner_kernel(pieces, z_size, place, near, far, *refs):
    values, outs = refs[: 2 * pieces], refs[2 * pieces : 2 * pieces + z_size]
    token_rows = refs[2 * pieces + z_size]
    totals = refs[-1]
    sides = near.shape[0] // PAIR
    rows, tokens = near.shape[2:]
    half = values[0].shape[1]
    for n, source in enumerate((near, far)):
        for m in range(PAIR):
            columns = jnp.concatenate(
                [
                    source[(x + m) % PAIR * sides + y].reshape(z_size * rows, tokens)
                    for y in range(sides)
                    for x in range(PAIR)
                ],
                axis=1,
            )
            blocks = values[m * pieces + n * sides : m * pieces + (n + 1) * sides]
            product = jnp.dot(
                columns,
                jnp.concatenate([ref[...] for ref in blocks], axis=0),
                preferred_element_type=jnp.float32,
            )
            part = slice(m * half, (m + 1) * half)
            totals[:, part] = product if n == 0 else totals[:, part] + product
    flag = place[1] == 0
    for x in range(PAIR):
        for y in range(sides):
            low = values[y][x * tokens : (x + 1) * tokens, :]
            high = values[pieces + y][(1 - x) * tokens : (2 - x) * tokens, :]
            at = (x * sides + y) * tokens
            token_rows[at : at + tokens, :half] = jnp.where(flag, low, high)
            token_rows[at : at + tokens, half:] = jnp.where(flag, high, low)
    for k, out in enumerate(outs):
        at = place[0] + k
        start = pl.multiple_of(jnp.where(at >= z_size, at - z_size, at) * rows, rows)
        out[...] = totals[pl.ds(start, rows), :].astype(jnp.bfloat16)


def plain_owner_products(place, near, far, first, second):
    z_size, rows, tokens = near.shape[1:]
    sides = near.shape[0] // PAIR
    halves = []
    for m, blocks in enumerate((first, second)):
        total = 0.0
        for n, array in enumerate((near, far)):
            order = [(x + m) % PAIR * sides + y for y in range(sides) for x in range(PAIR)]
            columns = jnp.stack([array[at] for at in order], axis=2)
            total = total + jnp.dot(
                columns.reshape(z_size * rows, -1),
                jnp.concatenate(blocks[n * sides : (n + 1) * sides], axis=0),
                preferred_element_type=jnp.float32,
            )
        halves.append(total.astype(jnp.bfloat16))
    every = jnp.concatenate(halves, axis=1).reshape(z_size, rows, -1)
    groups = []
    for x in range(PAIR):
        for y in range(sides):
            low = first[y][x * tokens : (x + 1) * tokens]
            high = second[y][(1 - x) * tokens : (2 - x) * tokens]
            groups.append(
                jnp.where(
                    place[1] == 0,
                    jnp.concatenate([low, high], axis=1),
                    jnp.concatenate([high, low], axis=1),
                )
            )
    return [cut(every, turned(place[0], k, z_size), 0) for k in range(z_size)] + [
        jnp.concatenate(groups, axis=0)
    ]


def owner_products(place, near, far, first, second):
    z_size, rows, tokens = near.shape[1:]
    if rows % 16:
        return plain_owner_products(place, near, far, first, second)
    pieces = len(first)
    width = 2 * first[0].shape[1]
    whole = pl.BlockSpec(memory_space=pltpu.VMEM)
    shape = jax.ShapeDtypeStruct((rows, width), jnp.bfloat16)
    return pl.pallas_call(
        functools.partial(owner_kernel, pieces, z_size),
        in_specs=[pl.BlockSpec(memory_space=pltpu.SMEM)] + [whole] * (2 + 2 * pieces),
        out_specs=[whole] * (z_size + 1),
        out_shape=[shape] * z_size
        + [jax.ShapeDtypeStruct((near.shape[0] * tokens, width), jnp.bfloat16)],
        scratch_shapes=[
            pltpu.VMEM((z_size * rows, width), jnp.float32),
        ],
        compiler_params=ROOM,
        cost_estimate=pl.CostEstimate(
            flops=4 * near.size * width, bytes_accessed=8 * near.size, transcendentals=0
        ),
    )(place, near, far, *first, *second)


def row_kernel(z_size, groups, place, token_rows, *refs):
    proj, outs = refs[:4], refs[4 : 4 + groups]
    rows_all, sems = refs[-2:]
    rows, tok_rows = proj[0].shape[1], outs[0].shape[0]
    copies = []
    for k, bits in enumerate(flips(z_size)):
        for c in range(2):
            at_core = place[3] if c == 0 else 1 - place[3]
            start = ((place[0] ^ bits) * 2 + at_core) * rows
            group, at = divmod(k, z_size // 2)
            copies.append(
                pltpu.make_async_copy(
                    proj[2 * c + group].at[at],
                    rows_all.at[pl.ds(pl.multiple_of(start, rows), rows), :],
                    sems.at[2 * k + c],
                )
            )
    for copy in copies:
        copy.start()
    for copy in copies:
        copy.wait()
    product = lax.dot_general(
        token_rows[...],
        rows_all[...],
        (((1,), (1,)), ((), ())),
        preferred_element_type=jnp.float32,
    ).astype(jnp.bfloat16)
    for n, out in enumerate(outs):
        out[...] = product[n * tok_rows : (n + 1) * tok_rows]


def plane_kernel(place, columns, *outs):
    y_size = columns.shape[2]
    for x in range(PAIR):
        for y in range(y_size):
            at_x, at_y = place[1] + x, place[2] + y
            at_x = jnp.where(at_x >= PAIR, at_x - PAIR, at_x)
            at_y = jnp.where(at_y >= y_size, at_y - y_size, at_y)
            out = outs[x * y_size + y]
            for z in range(columns.shape[0]):
                out[z] = columns[z, at_x, at_y]


def core_kernel(place, *refs):
    pieces, (near, far) = refs[:-2], refs[-2:]
    for n, piece in enumerate(pieces):
        for z in range(piece.shape[0]):
            near[n, z] = piece[z, place[3]]
            far[n, z] = piece[z, 1 - place[3]]


def sliced(kernel, place, arrays, shapes):
    whole = pl.BlockSpec(memory_space=pltpu.VMEM)
    return pl.pallas_call(
        kernel,
        in_specs=[pl.BlockSpec(memory_space=pltpu.SMEM)] + [whole] * len(arrays),
        out_specs=[whole] * len(shapes),
        out_shape=[jax.ShapeDtypeStruct(shape, jnp.bfloat16) for shape in shapes],
        compiler_params=ROOM,
        cost_estimate=pl.CostEstimate(
            flops=0,
            bytes_accessed=4 * sum(math.prod(shape) for shape in shapes),
            transcendentals=0,
        ),
    )(place, *arrays)


def by_place(blocks, index):
    size = len(blocks)
    back = jnp.stack([blocks[-k % size] for k in range(size)])
    start = jnp.where(index == 0, 0, size - index)
    return lax.dynamic_slice_in_dim(jnp.concatenate([back, back], axis=0), start, size, 0)


def plain_row_products(place, token_rows, groups, proj):
    width = proj[0].shape[2]
    z_size = 2 * proj[0].shape[0]
    cores = by_place(
        [jnp.concatenate(proj[2 * c : 2 * c + 2], axis=0) for c in range(2)], place[3]
    )
    order = {bits: k for k, bits in enumerate(flips(z_size))}
    along = jnp.stack([cores[:, order[k]] for k in range(z_size)])
    along = jnp.take(along, jnp.arange(z_size, dtype=jnp.int32) ^ place[0], axis=0)
    every = along.reshape(-1, width)
    product = jnp.dot(token_rows, every.T, preferred_element_type=jnp.float32)
    return jnp.split(product.astype(jnp.bfloat16), groups)


def row_products(place, token_rows, groups, proj):
    _, rows, width = proj[0].shape
    z_size = 2 * proj[0].shape[0]
    tok_rows = token_rows.shape[0] // groups
    cols = 2 * z_size * rows
    if rows % 16 or cols % 128:
        return plain_row_products(place, token_rows, groups, proj)
    whole = pl.BlockSpec(memory_space=pltpu.VMEM)
    shape = jax.ShapeDtypeStruct((tok_rows, cols), jnp.bfloat16)
    return pl.pallas_call(
        functools.partial(row_kernel, z_size, groups),
        in_specs=[pl.BlockSpec(memory_space=pltpu.SMEM), whole]
        + [pl.BlockSpec(memory_space=pl.ANY)] * len(proj),
        out_specs=[whole] * groups,
        out_shape=[shape] * groups,
        scratch_shapes=[
            pltpu.VMEM((cols, width), jnp.bfloat16),
            pltpu.SemaphoreType.DMA((2 * z_size,)),
        ],
        compiler_params=ROOM,
        cost_estimate=pl.CostEstimate(
            flops=2 * groups * tok_rows * width * cols,
            bytes_accessed=2 * cols * (width + groups * tok_rows),
            transcendentals=0,
        ),
    )(place, token_rows, *proj)


def final_kernel(z_size, place, *refs):
    pieces, out = refs[:-1], refs[-1]
    cols = pieces[0].shape[1] // z_size
    flags = place[1] == 0, place[2] == 0
    for z in range(z_size):
        part = slice(z * cols, (z + 1) * cols)
        near = [jnp.where(flags[1], pieces[y][:, part], pieces[1 - y][:, part]) for y in (0, 1)]
        far = [
            jnp.where(flags[1], pieces[2 + y][:, part], pieces[3 - y][:, part]) for y in (0, 1)
        ]
        near, far = jnp.concatenate(near, axis=1), jnp.concatenate(far, axis=1)
        wide = 2 * cols
        out[:, 2 * z * wide : (2 * z + 1) * wide] = jnp.where(flags[0], near, far)
        out[:, (2 * z + 1) * wide : (2 * z + 2) * wide] = jnp.where(flags[0], far, near)


def assembled(place, pieces, z_size):
    tokens = pieces[0].shape[0]
    y_size = len(pieces) // PAIR
    cols = pieces[0].shape[1] // z_size
    if y_size != 2 or 2 * cols % 128:
        split = [piece.reshape(tokens, z_size, cols) for piece in pieces]
        both = []
        for x in range(PAIR):
            found = jnp.stack(split[x * y_size : (x + 1) * y_size])
            start = jnp.where(place[2] == 0, 0, y_size - place[2])
            both.append(
                lax.dynamic_slice_in_dim(
                    jnp.concatenate([found, found], axis=0), start, y_size, 0
                )
            )
        both = jnp.stack(both)
        both = jnp.where(place[1] == 0, both, both[::-1])
        return both.transpose(2, 3, 0, 1, 4).reshape(tokens, -1)
    steps = 2 if tokens % 64 == 0 else 1

    def rows(array_cols):
        return pl.BlockSpec((tokens // steps, array_cols), lambda i, place: (i, 0))

    return pl.pallas_call(
        functools.partial(final_kernel, z_size),
        grid_spec=pltpu.PrefetchScalarGridSpec(
            num_scalar_prefetch=1,
            grid=(steps,),
            in_specs=[rows(z_size * cols)] * len(pieces),
            out_specs=rows(len(pieces) * z_size * cols),
        ),
        out_shape=jax.ShapeDtypeStruct((tokens, len(pieces) * z_size * cols), jnp.bfloat16),
        compiler_params=ROOM,
        cost_estimate=pl.CostEstimate(
            flops=0, bytes_accessed=4 * tokens * len(pieces) * z_size * cols, transcendentals=0
        ),
    )(place, *pieces)


def adam_rows(old_rows, grad_rows, first_moment, second_moment):
    first = decay_first * first_moment.astype(jnp.float32) + (1.0 - decay_first) * grad_rows
    second = (
        decay_second * second_moment.astype(jnp.float32)
        + (1.0 - decay_second) * grad_rows * grad_rows
    )
    weight_now = old_rows.astype(jnp.float32)
    update = (
        first / bias_first / (jnp.sqrt(second / bias_second) + adam_eps) + weight_decay * weight_now
    )
    return (
        (weight_now - step_rate * update).astype(jnp.bfloat16),
        first.astype(jnp.bfloat16),
        second.astype(jnp.bfloat16),
    )


def adam_kernel(place, count, *refs):
    pieces, (old_rows, first_moment, second_moment), outs = refs[:count], refs[count:-3], refs[-3:]
    grad = pieces[0][...].astype(jnp.float32)
    for piece in pieces[1:]:
        grad = grad + piece[...].astype(jnp.float32)
    mid = grad.shape[1] // 2
    swap = jnp.concatenate([grad[:, mid:], grad[:, :mid]], axis=1)
    grad = jnp.where(place[1] == 0, grad, swap)
    for out, value in zip(
        outs, adam_rows(old_rows[...], grad, first_moment[...], second_moment[...])
    ):
        out[...] = value


def adam_step(place, pieces, old_rows, first_moment, second_moment):
    arrays = [*pieces, old_rows, first_moment, second_moment]
    whole = pl.BlockSpec(memory_space=pltpu.VMEM)
    return pl.pallas_call(
        lambda place, *refs: adam_kernel(place, len(pieces), *refs),
        in_specs=[pl.BlockSpec(memory_space=pltpu.SMEM)] + [whole] * len(arrays),
        out_specs=[whole] * 3,
        out_shape=[jax.ShapeDtypeStruct(old_rows.shape, jnp.bfloat16)] * 3,
        compiler_params=ROOM,
        cost_estimate=pl.CostEstimate(
            flops=40 * old_rows.size,
            bytes_accessed=2 * (len(arrays) + 3) * old_rows.size,
            transcendentals=old_rows.size,
        ),
    )(place, *arrays)


def shift(value, axis, step, wrap=True):
    size = lax.axis_size(axis)
    pairs = [(i, (i + step) % size) for i in range(size) if wrap or 0 <= i + step < size]
    return lax.ppermute(value, axis, pairs)


def turned(index, step, size):
    moved = index + step
    return jnp.where(moved >= size, moved - size, moved)


def z_bits(z_size):
    assert z_size & (z_size - 1) == 0
    return [1 << n for n in range(z_size.bit_length() - 2, -1, -1)]


def flips(z_size):
    bits = z_bits(z_size)
    return [
        functools.reduce(int.__xor__, [bit for n, bit in enumerate(bits) if k >> n & 1], 0)
        for k in range(z_size)
    ]


def cut(value, index, dim):
    return lax.dynamic_index_in_dim(value, index, dim, keepdims=False)


def step(
    attn_inputs,
    queries,
    key_vectors,
    logp_grad,
    new_logp,
    old_logp,
    rewards,
    group_ids,
    lengths,
    value_proj,
    first_moment,
    second_moment,
):
    z_size, y_size, core_size = lax.axis_size("z"), lax.axis_size("y"), lax.axis_size("core")
    z_index, x_index = lax.axis_index("z"), lax.axis_index("x")
    side_index = lax.axis_index("y") * core_size + lax.axis_index("core")
    tok_rows, _ = attn_inputs.shape
    half = tok_rows // ROLLS
    full_len = half * z_size * PAIR
    shard_rows = first_moment.shape[0]
    y_index, core_index = lax.axis_index("y"), lax.axis_index("core")
    place = jnp.stack([z_index, x_index, y_index, core_index]).astype(jnp.int32)

    key_room, key_out, q_out, g_out = packed(key_vectors, queries, logp_grad)
    key_far = shift(key_out, "x", 1)
    q_far = shift(q_out, "x", 1)
    g_far = shift(g_out, "x", 1)
    key_block = lax.dynamic_update_slice(key_room, key_far, (tok_rows, 0))
    key_blocks = [key_block] + [shift(key_block, "z", k, False) for k in range(1, z_size)]
    columns = attn_inputs.T.reshape(z_size, PAIR, y_size, core_size, shard_rows, tok_rows)
    found = []
    block = (z_size, core_size, shard_rows, tok_rows)
    cuts = sliced(plane_kernel, place, [columns], [block] * (PAIR * y_size))
    for x in range(PAIR):
        for k in range(y_size):
            piece = cuts[x * y_size + k]
            if x or k:
                pairs = [
                    (a * y_size + b, (a + x) % PAIR * y_size + (b + k) % y_size)
                    for a in range(PAIR)
                    for b in range(y_size)
                ]
                piece = lax.ppermute(piece, ("x", "y"), pairs)
            found.append(piece)
    every = (PAIR * y_size, z_size, shard_rows, tok_rows)
    near_cols, far_cols = sliced(core_kernel, place, found, [every] * 2)
    far_cols = shift(far_cols, "core", 1)

    coeff = coefficients(
        place, rewards, group_ids, lengths, new_logp, old_logp, full_len
    )
    coeff_far = shift(coeff, "x", 1)

    own_proj = lax.dynamic_slice_in_dim(value_proj, side_index * shard_rows, shard_rows, 0)
    own_proj = lax.optimization_barrier(own_proj)
    bits = z_bits(z_size)
    known = own_proj[None]
    for n, bit in enumerate(bits):
        pairs = [(i, i ^ bit) for i in range(z_size)]
        arrived = lax.ppermute(known, "z", pairs)
        if n < len(bits) - 1:
            known = jnp.concatenate([known, arrived], axis=0)
    proj = [known, arrived, shift(known, "core", 1), shift(arrived, "core", 1)]

    parts = attention_parts(place, queries, q_far, logp_grad, g_far, coeff, coeff_far, key_blocks)
    total = parts[0].astype(jnp.float32)
    for k in range(1, z_size):
        arrived = shift(parts[k], "z", -k, False)
        total = total + arrived.astype(jnp.float32)

    def over_sides(value):
        found = [value] + [shift(value, "y", k) for k in range(1, y_size)]
        return found + [shift(block, "core", 1) for block in found]

    first_cols = total.astype(jnp.bfloat16)
    second_cols = shift(first_cols, "x", 1)
    first_all = over_sides(first_cols)
    second_all = over_sides(second_cols)

    pieces = owner_products(place, near_cols, far_cols, first_all, second_all)
    arrived_sums = [shift(pieces[k], "z", k) for k in range(1, z_size)]
    products = row_products(place, pieces[z_size], PAIR * y_size, proj)
    back = list(products)
    for k in range(1, y_size):
        back[k] = shift(products[k], "y", -k)
    back[y_size] = shift(products[y_size], "x", 1)
    for k in range(1, y_size):
        pairs = [
            (x * y_size + y, (1 - x) * y_size + (y - k) % y_size)
            for x in range(PAIR)
            for y in range(y_size)
        ]
        back[y_size + k] = lax.ppermute(products[y_size + k], ("x", "y"), pairs)
    input_grad = assembled(place, back, z_size)

    new_rows, new_first, new_second = adam_step(
        place, [pieces[0], *arrived_sums], own_proj, first_moment, second_moment
    )
    sides = [new_rows] + [shift(new_rows, "y", k) for k in range(1, y_size)]
    others = [shift(block, "core", 1) for block in sides]
    if y_size == 2:
        columns = [
            [jnp.where(y_index == 0, blocks[y], blocks[1 - y]) for y in range(2)]
            for blocks in (sides, others)
        ]
    else:
        columns = [list(by_place(blocks, y_index)) for blocks in (sides, others)]
    new_proj = jnp.concatenate(
        [
            jnp.where(core_index == c, columns[0][y], columns[1][y])
            for y in range(y_size)
            for c in range(core_size)
        ],
        axis=0,
    )
    return (input_grad, new_proj, new_first, new_second)


def solution(mesh):
    fsdp_size, side_size = mesh.shape["fsdp"], mesh.shape["side"]
    fine = Mesh(
        mesh.devices.reshape(fsdp_size // PAIR, PAIR, side_size // 2, 2),
        ("z", "x", "y", "core"),
    )
    tokens = ("y", "core", "z", "x")
    placed = (
        P(tokens, None),
        P(tokens, None),
        P(tokens, None),
        P(tokens, None),
        P(tokens),
        P(tokens),
        P(),
        P(),
        P(),
        P(("z", "x"), None),
        P(("z", "x", "y", "core"), None),
        P(("z", "x", "y", "core"), None),
    )
    return jax.shard_map(
        step,
        mesh=fine,
        in_specs=placed,
        out_specs=(
            P(tokens, None),
            P(("z", "x"), None),
            P(("z", "x", "y", "core"), None),
            P(("z", "x", "y", "core"), None),
        ),
        check_vma=False,
    )
```
